32 devices in a mesh: dp: 16 (over z, y, x), tensor: 2 (over core).
Axes of the slice: x: 2, y: 2, z: 4, core: 2. Of those that a mesh axis runs over, the one named last changes fastest.
Arguments:
- pool: bfloat16 [4096, 2048], P('dp', 'tensor'), may hold values from -6 to 6
- select: int32 [2048], P('dp'), may hold values from 0 to 4095, as said below
- reward_w: bfloat16 [2048], P('tensor'), may hold values from -0.125 to 0.125
- routes: int32 [2048, 6], P('dp'), may hold values from 0 to 15, all different within a row; in each aligned block of 128 rows (0 to 127, 128 to 255, ...) at most 60 rows name the same one
- gates: float32 [2048, 6], P('dp'), may hold values from 0.05 to 0.5
- target: bfloat16 [2048, 2048], P('dp', 'tensor'), may hold values from -6 to 6
- w_gate: bfloat16 [16, 1408, 2048], P('dp', 'tensor'), may hold values from -0.125 to 0.125
- w_up: bfloat16 [16, 1408, 2048], P('dp', 'tensor'), may hold values from -0.125 to 0.125
- w_down: bfloat16 [16, 1408, 2048], P('dp', 'tensor'), may hold values from -0.15625 to 0.15625
Outputs:
- mixed: bfloat16 [2048, 2048], P('dp', 'tensor')
- grad_gate: bfloat16 [16, 1408, 2048], P('dp', 'tensor')
- grad_up: bfloat16 [16, 1408, 2048], P('dp', 'tensor')
- grad_down: bfloat16 [16, 1408, 2048], P('dp', 'tensor')
The draws below stay inside these ranges and needn't reach their ends.
Inputs may be any that keep to these rules, and one draw needn't show every extreme that they name: The 128 entries of aligned block i of select are distinct rows of pool's block i, rows i * 256 to (i + 1) * 256 - 1. `routes`: each row names 6 different experts. In the 128 rows of one device no expert is named more than 60 times, a bound that some block reaches.
All inputs are finite; a program needn't handle non-finite values.
Results may differ from the reference program's by a relative error of at most 0.015.
Values may be sent and summed in bfloat16 or wider, within the bound.
A program may use at most 128 MiB of HBM per device.

```python
import math
import jax
import jax.numpy as jnp
import numpy as np
from jax import lax

D = 2048
FF = 1408
TOPK = 6
SEL_DEV = 128
POOL_DEV = 256
EXPERTS = 16
CAP = 60
SEL = 2048
POOL = 4096
N_TENSOR = 2


def draw_select(key, part):
    block_count = SEL // SEL_DEV

    def one_block(block_key):
        first_key, second_key, third_key = jax.random.split(block_key, 3)
        inner = jax.random.permutation(first_key, POOL_DEV - 2)[:SEL_DEV].astype(jnp.int32) + 1
        lowest = jax.random.randint(second_key, (), 0, SEL_DEV)
        highest = (lowest + 1 + jax.random.randint(third_key, (), 0, SEL_DEV - 1)) % SEL_DEV
        inner = inner.at[lowest].set(0)
        inner = inner.at[highest].set(POOL_DEV - 1)
        return inner.astype(jnp.int32)
    block_keys = jax.random.split(jax.random.fold_in(key, 11), block_count)
    local_rows = jax.vmap(one_block)(block_keys)
    offsets = jnp.arange(block_count, dtype=jnp.int32)[:, None] * POOL_DEV
    return (local_rows + offsets).reshape(SEL).astype(jnp.int32)


def levels(rng, shape, cuts, low, high):
    loudness, own = 1.0, jax.random.fold_in(rng, 6)
    for position, blocks in cuts:
        heights = jnp.exp(jax.random.uniform(jax.random.fold_in(own, position), (blocks,), jnp.float32, low / len(cuts), high / len(cuts)))
        loudness = loudness * jnp.repeat(heights, shape[position] // blocks).reshape([-1 if axis == position else 1 for axis in range(len(shape))])
    return loudness


def deal_out(own_key, own, number, rows, count, top, bound, skew):
    sequence = jax.random.permutation(own_key, count)
    packed, ordinary = shares(count, rows * top, bound, skew, True), shares(count, rows * top, bound, skew, False)
    places = jnp.arange(count)

    def named(sizes, turn):
        used = int((sizes > 0).sum())
        fixed = max(1, used // 4)
        moved = fixed + (places - fixed + turn * (used - fixed)) % max(1, count - fixed)
        return jnp.zeros((count,), jnp.int32).at[sequence[jnp.where(places < fixed, places, moved)]].set(jnp.asarray(sizes, jnp.int32))

    sizes = jnp.where(number % 4 == 0, named(packed, number // 4), named(ordinary, number - number // 4 - 1))
    mixed = jax.random.permutation(jax.random.fold_in(own, 3), count)
    donor, receiver = mixed[0:count // 2 * 2:2], mixed[1:count // 2 * 2:2]
    slack = jnp.minimum(sizes[donor] - 1, bound - sizes[receiver]) // 2
    slack = jnp.where((donor == sequence[0]) | (receiver == sequence[0]) | (sizes[receiver] == 0), 0, jnp.maximum(slack, 0))
    moved = jax.random.randint(jax.random.fold_in(own, 4), (count // 2,), 0, 1 << 20) % (slack + 1)
    sizes = sizes.at[donor].add(-moved).at[receiver].add(moved)
    members = jnp.searchsorted(jnp.cumsum(sizes), jnp.arange(rows * top), side="right").astype(jnp.int32)
    grid = members.reshape(top, rows).T
    grid = grid[jax.random.permutation(jax.random.fold_in(own, 1), rows)]
    turn = jax.random.randint(jax.random.fold_in(own, 2), (rows, 1), 0, top)
    return jnp.take_along_axis(grid, (jnp.arange(top)[None, :] + turn) % top, axis=1)


def shares(count, total, limit, skew, full):
    weights = [(1 << 20) // math.isqrt(rank ** skew) + 1 for rank in range(1, count + 1)]
    largest = limit if full else min(limit, max(-(-total // count), total * weights[0] // sum(weights)))
    least = 1 if total - largest >= count - 1 else 0
    holding, spare = [largest] + [least] * (count - 1), total - largest - least * (count - 1)
    while spare > 0:
        free = [i for i in range(1, count) if holding[i] < largest] or [i for i in range(1, count) if holding[i] < limit]
        mass, left = sum([weights[i] for i in free]), spare
        for i in free:
            more = min(limit - holding[i], max(1, left * weights[i] // mass), spare)
            holding[i] = holding[i] + more
            spare = spare - more
    return np.array(holding)


def scatter_about(key, dims, scale, reach, shards=(), kind=jnp.bfloat16):
    drawn = scale * jax.random.normal(key, dims, jnp.float32)
    if shards:
        drawn = drawn * levels(key, dims, shards, -0.22, 0.18)
    return jnp.clip(drawn, -reach, reach).astype(kind)


def setup_inputs(seed: int = 0) -> dict:
    key_list = jax.random.split(jax.random.key(seed), 10)
    pool = scatter_about(key_list[0], (POOL, D), 1.0, 6.0, ((0, 16), (1, 2)))
    select = draw_select(jax.random.fold_in(key_list[9], 71), 0)
    reward_w = scatter_about(key_list[2], (D,), D ** -0.5, 0.125, ((0, 2),))
    routes_keys = jax.random.split(jax.random.fold_in(key_list[3], 1), SEL // SEL_DEV)
    routes_turns = jax.random.permutation(jax.random.fold_in(key_list[3], 3), SEL // SEL_DEV)
    routes = jax.vmap(lambda own, number: deal_out(jax.random.fold_in(key_list[3], 2), own, number, SEL_DEV, EXPERTS, TOPK, CAP, 2))(routes_keys, routes_turns).reshape((SEL, TOPK))
    gates = jnp.clip(jnp.exp(math.log(0.5) - 2.3025851 * jax.random.uniform(key_list[4], (SEL, TOPK), jnp.float32) ** levels(key_list[4], (SEL, TOPK), ((0, 16),), -0.2, 0.2)), 0.05, 0.5)
    target = scatter_about(key_list[5], (SEL, D), 1.0, 6.0, ((0, 16), (1, 2)))
    w_gate = scatter_about(key_list[6], (EXPERTS, FF, D), D ** -0.5, 0.125, ((0, 16), (1, 2)))
    w_up = scatter_about(key_list[7], (EXPERTS, FF, D), D ** -0.5, 0.125, ((0, 16), (1, 2)))
    w_down = scatter_about(key_list[8], (EXPERTS, FF, D), FF ** -0.5, 0.15625, ((0, 16), (1, 2)))
    return {"pool": pool, "select": select, "reward_w": reward_w, "routes": routes, "gates": gates, "target": target, "w_gate": w_gate, "w_up": w_up, "w_down": w_down}


def reference(pool, select, reward_w, routes, gates, target, w_gate, w_up, w_down):
    chosen = pool[select]
    reward = jnp.dot(chosen, reward_w, preferred_element_type=jnp.float32)
    keep_scale = jax.nn.sigmoid(reward)
    route_cot = ((keep_scale[:, None] * gates)[:, :, None] * target.astype(jnp.float32)[:, None, :]).astype(jnp.bfloat16)
    cot_flat = route_cot.reshape(SEL * TOPK, D)
    block_count = SEL // SEL_DEV
    flat_routes = routes.reshape(block_count, SEL_DEV * TOPK)
    onehot = (flat_routes[:, :, None] == jnp.arange(EXPERTS, dtype=jnp.int32)[None, None, :]).astype(jnp.int32)
    slot_rank = jnp.sum((jnp.cumsum(onehot, axis=1) - onehot) * onehot, axis=2)
    column = (jnp.arange(block_count, dtype=jnp.int32)[:, None] * CAP + slot_rank).astype(jnp.int32)
    route_ids = jnp.arange(SEL * TOPK, dtype=jnp.int32).reshape(block_count, SEL_DEV * TOPK)
    slot_table = jnp.full((EXPERTS, block_count * CAP), SEL * TOPK, jnp.int32).at[flat_routes, column].set(route_ids)

    def expert(operands):
        slot_ids, gate_mat, up_mat, down_mat = operands
        live_rows = slot_ids < SEL * TOPK
        safe_ids = jnp.where(live_rows, slot_ids, 0)
        expert_rows = chosen[safe_ids // TOPK] * live_rows[:, None].astype(chosen.dtype)
        expert_cot = cot_flat[safe_ids] * live_rows[:, None].astype(cot_flat.dtype)
        gate_act = jnp.dot(expert_rows, gate_mat.T, preferred_element_type=jnp.float32)
        up_act = jnp.dot(expert_rows, up_mat.T, preferred_element_type=jnp.float32)
        sigmoid_gate = jax.nn.sigmoid(gate_act)
        hidden = (jax.nn.silu(gate_act) * up_act).astype(jnp.bfloat16)
        grouped = hidden.reshape(-1, N_TENSOR, FF // N_TENSOR).astype(jnp.float32)
        down_groups = down_mat.reshape(N_TENSOR, FF // N_TENSOR, D).astype(jnp.float32)
        group_sums = jnp.einsum("rgf,gfd->grd", grouped, down_groups)
        rounded = lax.optimization_barrier(group_sums.astype(jnp.bfloat16))
        expert_out = jnp.sum(rounded.astype(jnp.float32), axis=0).astype(jnp.bfloat16)
        hidden_grad = jnp.dot(expert_cot, down_mat.T, preferred_element_type=jnp.float32)
        gate_grad = (hidden_grad * up_act * sigmoid_gate * (1.0 + gate_act * (1.0 - sigmoid_gate))).astype(jnp.bfloat16)
        up_grad = (hidden_grad * jax.nn.silu(gate_act)).astype(jnp.bfloat16)
        grad_down = jnp.dot(hidden.T, expert_cot, preferred_element_type=jnp.float32).astype(jnp.bfloat16)
        grad_gate = jnp.dot(gate_grad.T, expert_rows, preferred_element_type=jnp.float32).astype(jnp.bfloat16)
        grad_up = jnp.dot(up_grad.T, expert_rows, preferred_element_type=jnp.float32).astype(jnp.bfloat16)
        return expert_out, grad_gate, grad_up, grad_down

    outputs, grad_gate, grad_up, grad_down = lax.map(expert, (slot_table, w_gate, w_up, w_down))
    route_out = outputs[flat_routes, column].reshape(SEL, TOPK, D).astype(jnp.float32)
    mixed = jnp.sum(route_out * gates[:, :, None], axis=1).astype(jnp.bfloat16)
    return mixed, grad_gate, grad_up, grad_down
```

```python
import functools
import jax
import jax.numpy as jnp
from jax import lax
from jax.experimental import pallas as pl
from jax.experimental.pallas import tpu as pltpu
from jax.sharding import PartitionSpec as P

MESH = pl.DeviceIdType.MESH
PLANE = 4
F32 = jnp.float32
BF16 = jnp.bfloat16


def slot_factor(route_hit, weights):
    return jnp.sum(jnp.where(route_hit, weights.reshape(-1)[:, None], 0.0), axis=0)


def generic(pool, select, reward_w, routes, gates, target, w_gate, w_up, w_down):
    pool_rows = pool.shape[0]
    local_rows = select - lax.axis_index("dp") * pool_rows
    chosen = jnp.take(pool, local_rows, axis=0)
    sel_rows, top_count = routes.shape
    owners = lax.axis_size("dp")
    exp_dev = w_gate.shape[0]
    experts = owners * exp_dev
    capacity = 5 * sel_rows * top_count // (4 * experts)
    slot_count = experts * capacity
    flat_routes = routes.reshape(-1)
    onehot = (flat_routes[:, None] == jnp.arange(experts, dtype=jnp.int32)[None, :]).astype(
        jnp.int32
    )
    before = jnp.cumsum(onehot, axis=0) - onehot
    slot_rank = jnp.sum(before * onehot, axis=1)
    slot_place = flat_routes * capacity + slot_rank
    route_hit = slot_place[:, None] == jnp.arange(slot_count, dtype=jnp.int32)[None, :]
    route_pick = route_hit.astype(jnp.bfloat16).reshape(sel_rows, top_count, slot_count)
    token_pick = jnp.sum(route_pick, axis=1)
    reward = lax.psum(jnp.dot(chosen, reward_w, preferred_element_type=jnp.float32), "tensor")
    keep_scale = jax.nn.sigmoid(reward)
    slot_scale = slot_factor(route_hit, keep_scale[:, None] * gates)
    token_send = jnp.einsum(
        "sp,sd->pd", token_pick, chosen, preferred_element_type=jnp.float32
    ).astype(jnp.bfloat16)
    picked_target = jnp.einsum("sp,sd->pd", token_pick, target, preferred_element_type=jnp.float32)
    cot_send = (picked_target * slot_scale[:, None]).astype(jnp.bfloat16)
    token_part, cot_part = (
        lax.all_to_all(token_send, "dp", split_axis=0, concat_axis=0, tiled=True),
        lax.all_to_all(cot_send, "dp", split_axis=0, concat_axis=0, tiled=True),
    )
    received_tokens, received_cots = (
        lax.all_gather(token_part, "tensor", axis=1, tiled=True),
        lax.all_gather(cot_part, "tensor", axis=1, tiled=True),
    )
    width = received_tokens.shape[1]
    token_rows = received_tokens.reshape(owners, exp_dev, capacity, width)
    cot_rows = received_cots.reshape(owners, exp_dev, capacity, width)
    gate_act = jnp.einsum("secd,efd->secf", token_rows, w_gate, preferred_element_type=jnp.float32)
    up_act = jnp.einsum("secd,efd->secf", token_rows, w_up, preferred_element_type=jnp.float32)
    sigmoid_gate = jax.nn.sigmoid(gate_act)
    hidden = (gate_act * sigmoid_gate * up_act).astype(jnp.bfloat16)
    partial_value = jnp.einsum("secf,efd->secd", hidden, w_down, preferred_element_type=jnp.float32)
    summed = lax.psum_scatter(
        partial_value.astype(jnp.bfloat16), "tensor", scatter_dimension=3, tiled=True
    )
    returned = lax.all_to_all(summed, "dp", split_axis=0, concat_axis=0, tiled=True).reshape(
        slot_count, -1
    )
    route_rows = jnp.einsum("skp,pd->skd", route_pick, returned, preferred_element_type=jnp.float32)
    mixed = jnp.sum(route_rows * gates[:, :, None], axis=1).astype(jnp.bfloat16)
    hidden_grad = jnp.einsum("secd,efd->secf", cot_rows, w_down, preferred_element_type=jnp.float32)
    gate_grad = (
        hidden_grad * up_act * sigmoid_gate * (1.0 + gate_act * (1.0 - sigmoid_gate))
    ).astype(jnp.bfloat16)
    up_grad = (hidden_grad * gate_act * sigmoid_gate).astype(jnp.bfloat16)
    grad_down = jnp.einsum(
        "secf,secd->efd", hidden, cot_rows, preferred_element_type=jnp.float32
    ).astype(jnp.bfloat16)
    grad_gate = jnp.einsum(
        "secf,secd->efd", gate_grad, token_rows, preferred_element_type=jnp.float32
    ).astype(jnp.bfloat16)
    grad_up = jnp.einsum(
        "secf,secd->efd", up_grad, token_rows, preferred_element_type=jnp.float32
    ).astype(jnp.bfloat16)
    return (mixed, grad_gate, grad_up, grad_down)


def place(line):
    d = lax.axis_index("dp")
    c = lax.axis_index("tensor")
    z, q = d // PLANE, d % PLANE
    y, x = q // 2, q % 2
    mates = [((y + ry) % 2) * 2 + (x + rx) % 2 for ry, rx in ((0, 1), (1, 0), (1, 1))]
    return d, c, z, q, mates


def greet(d, c, z, q, mates, line):
    barrier = pltpu.get_barrier_semaphore()
    for m in mates:
        pl.semaphore_signal(barrier, inc=1, device_id=(z * PLANE + m, c), device_id_type=MESH)
    pl.semaphore_signal(barrier, inc=1, device_id=(d, 1 - c), device_id_type=MESH)

    @pl.when(z > 0)
    def _():
        pl.semaphore_signal(barrier, inc=1, device_id=(d - PLANE, c), device_id_type=MESH)

    @pl.when(z < line - 1)
    def _():
        pl.semaphore_signal(barrier, inc=1, device_id=(d + PLANE, c), device_id_type=MESH)

    below, above = (z + line - 1) // line, (2 * line - 2 - z) // line
    pl.semaphore_wait(barrier, 4 + below + above)


def remote(src, dst, send, recv, dev):
    return pltpu.make_async_remote_copy(
        src_ref=src, dst_ref=dst, send_sem=send, recv_sem=recv, device_id=dev, device_id_type=MESH
    )


def dispatch_kernel(
    line, pad, pool_ref, sel_ref, rw_ref, rt_ref, gt_ref, target_ref,
    rows0_ref, rows1_ref, side_ref,
    data, scale, part, part_in, stage,
    zsend, zrecv, ssend, srecv, csend, crecv, xsend, xrecv, tsend, trecv, psend, precv,
):
    d, c, z, q, mates = place(line)
    experts = line * PLANE
    sel_rows, half = target_ref.shape
    top = gt_ref.shape[0]
    rows = (rows0_ref, rows1_ref)
    mine = pl.ds(pl.multiple_of(c * half, half), half)

    hit = (
        lax.broadcasted_iota(jnp.int32, (sel_rows, pool_ref.shape[0]), 1) == sel_ref[...]
    ).astype(F32).astype(BF16)
    chosen = jnp.dot(hit, pool_ref[...], preferred_element_type=F32).astype(BF16)
    data[0, z] = chosen
    data[1, z] = target_ref[...]
    part[...] = lax.dot_general(
        rw_ref[...], chosen, (((1,), (1,)), ((), ())), preferred_element_type=F32
    )
    expert_id = lax.broadcasted_iota(jnp.int32, (experts, sel_rows), 0)
    member = jnp.zeros((experts, sel_rows), F32)
    gate = jnp.zeros((experts, sel_rows), F32)
    for k in range(top):
        eq = rt_ref[k : k + 1, :] == expert_id
        member = member + jnp.where(eq, 1.0, 0.0)
        gate = gate + jnp.where(eq, gt_ref[k : k + 1, :], 0.0)
    tri = jnp.where(
        lax.broadcasted_iota(jnp.int32, (sel_rows, sel_rows), 0)
        < lax.broadcasted_iota(jnp.int32, (sel_rows, sel_rows), 1),
        1.0,
        0.0,
    ).astype(BF16)
    before = jnp.dot(member.astype(BF16), tri, preferred_element_type=F32)
    side_ref[z, 0:experts, :] = jnp.where(member > 0.5, before, -1.0)
    side_ref[z, experts : 2 * experts, :] = gate

    greet(d, c, z, q, mates, line)
    partner = (d, 1 - c)
    reward_copy = remote(part, part_in, psend, precv, partner)
    reward_copy.start()

    def zcopies(a, s, way):
        blk = z - way * s
        dev = (d + way * PLANE, c)
        w = (way + 1) // 2
        main = remote(data.at[a, blk], data.at[a, blk], zsend.at[a, w, s], zrecv.at[a, blk], dev)
        if a == 0:
            extra = remote(
                side_ref.at[blk], side_ref.at[blk], ssend.at[w, s], srecv.at[blk], dev
            )
        else:
            extra = remote(scale.at[blk], scale.at[blk], csend.at[w, s], crecv.at[blk], dev)
        return extra, main

    def sends(a, s, way):
        blk, to = z - way * s, z + way
        return (blk >= 0) & (blk < line) & (to >= 0) & (to < line)

    def zstart(a, s):
        for way in (1, -1):
            @pl.when(sends(a, s, way))
            def _():
                for cp in zcopies(a, s, way):
                    cp.start()

    def arrives(s, way):
        blk = z - way * (s + 1)
        return (blk >= 0) & (blk < line)

    def zwait(a, s):
        for way in (1, -1):
            @pl.when(arrives(s, way))
            def _():
                blk = z - way * (s + 1)
                dev = (d, 1 - c)
                remote(
                    data.at[a, blk], data.at[a, blk], zsend.at[a, 0, 0], zrecv.at[a, blk], dev
                ).wait_recv()
                if a == 0:
                    remote(
                        side_ref.at[blk], side_ref.at[blk], ssend.at[0, 0], srecv.at[blk], dev
                    ).wait_recv()
                else:
                    remote(
                        scale.at[blk], scale.at[blk], csend.at[0, 0], crecv.at[blk], dev
                    ).wait_recv()

    def tcopy(a, b):
        place_ = rows[a].at[b, :, mine]
        return remote(place_, place_, tsend.at[a, b], trecv.at[a, b], partner)

    def xcopy(a, zp, r):
        return remote(
            stage.at[a, zp, r],
            rows[a].at[zp * PLANE + q, :, mine],
            xsend.at[a, zp, r],
            xrecv.at[a, zp * PLANE + q],
            (z * PLANE + mates[r], c),
        )

    slot_id = lax.broadcasted_iota(jnp.int32, (pad, sel_rows), 0).astype(F32)

    def process(a, zp):
        block = data[a, zp]
        for r in (0, 1, 2, 3):
            e = z * PLANE + (mates[r] if r < 3 else q)
            m = slot_id == side_ref[zp, pl.ds(e, 1), :]
            picked = jnp.dot(
                jnp.where(m, 1.0, 0.0).astype(BF16), block, preferred_element_type=F32
            )
            if a == 1:
                picked = picked * jnp.sum(
                    jnp.where(m, scale[zp, pl.ds(e, 1), :], 0.0), axis=1, keepdims=True
                )
            picked = picked.astype(BF16)
            if r < 3:
                stage[a, zp, r] = picked
                xcopy(a, zp, r).start()
            else:
                rows[a][zp * PLANE + q, :, mine] = picked
                tcopy(a, zp * PLANE + q).start()

    def forward(a, zp):
        for r in range(3):
            b = zp * PLANE + mates[r]
            remote(
                stage.at[a, zp, r], rows[a].at[b, :, mine], xsend.at[a, zp, r],
                xrecv.at[a, b], partner,
            ).wait_recv()
            tcopy(a, b).start()

    def got(fn, a, s):
        for way in (1, -1):
            @pl.when(arrives(s, way))
            def _():
                fn(a, z - way * (s + 1))

    zstart(0, 0)
    process(0, z)
    reward_copy.wait()
    keep = 1.0 / (1.0 + jnp.exp(-(part[0:1, :] + part_in[0:1, :])))
    scale[z] = keep * side_ref[z, experts : 2 * experts, :]
    last = line - 2
    for a in (0, 1):
        for s in range(line - 1):
            zwait(a, s)
            if s < last:
                zstart(a, s + 1)
            elif a == 0:
                zstart(1, 0)
            got(process, a, s)
            if s == 0:
                forward(a, z)
            else:
                got(forward, a, s - 1)
        if a == 0:
            process(1, z)
        got(forward, a, last)

    for a in (0, 1):
        for b in range(experts):
            tcopy(a, b).wait()
        for zp in range(line):
            for r in range(3):
                xcopy(a, zp, r).wait_send()
        for s in range(line - 1):
            for way in (1, -1):
                @pl.when(sends(a, s, way))
                def _():
                    for cp in zcopies(a, s, way):
                        cp.wait_send()


def return_kernel(
    line, pad, value_ref, side_ref, mixed_ref,
    partner_in, stage, plane_in, acc, out_stage, line_in,
    tsend, trecv, xsend, xrecv, zsend, zrecv,
):
    d, c, z, q, mates = place(line)
    experts = line * PLANE
    half = mixed_ref.shape[1]
    sel_rows = mixed_ref.shape[0]
    mine = pl.ds(pl.multiple_of(c * half, half), half)
    other = pl.ds(pl.multiple_of((1 - c) * half, half), half)
    partner = (d, 1 - c)
    turn = 2 * (z // (line // 2)) - 1

    def order(i):
        return (z + turn * (1 + i) + 2 * line) % line

    greet(d, c, z, q, mates, line)

    def tcopy(b):
        return remote(
            value_ref.at[b, :, other], partner_in.at[b], tsend.at[b], trecv.at[b], partner
        )

    def xcopy(zp, r):
        return remote(
            stage.at[zp, r], plane_in.at[zp, q], xsend.at[zp, r], xrecv.at[zp, q],
            (z * PLANE + mates[r], c),
        )

    for i in range(line):
        for r in (2, 0, 1, 3):
            tcopy(order(i) * PLANE + (mates[r] if r < 3 else q)).start()
    for i in range(line):
        zp = order(i)
        for r in (2, 0, 1, 3):
            b = zp * PLANE + (mates[r] if r < 3 else q)
            tcopy(b).wait_recv()
            total = (value_ref[b, :, mine].astype(F32) + partner_in[b].astype(F32)).astype(BF16)
            if r < 3:
                stage[zp, r] = total
                xcopy(zp, r).start()
            else:
                plane_in[zp, q] = total

    slot_id = lax.broadcasted_iota(jnp.int32, (pad, sel_rows), 0).astype(F32)

    def combine(zp):
        for r in range(3):
            remote(
                stage.at[zp, r], plane_in.at[zp, mates[r]], xsend.at[zp, r],
                xrecv.at[zp, mates[r]], partner,
            ).wait_recv()
        total = jnp.zeros((sel_rows, half), F32)
        for j in range(PLANE):
            e = z * PLANE + j
            w = jnp.where(
                slot_id == side_ref[zp, pl.ds(e, 1), :],
                side_ref[zp, pl.ds(experts + e, 1), :],
                0.0,
            )
            high = w.astype(BF16)
            low = (w - high.astype(F32)).astype(BF16)
            both = jnp.concatenate([high, low], axis=0)
            values = plane_in[zp, j]
            total = total + lax.dot_general(
                both, jnp.concatenate([values, values], axis=0),
                (((0,), (0,)), ((), ())), preferred_element_type=F32,
            )
        acc[zp] = total

    def zcopy(w, s):
        to = d + (2 * w - 1) * PLANE
        return remote(
            out_stage.at[w, s], line_in.at[w, s], zsend.at[w, s], zrecv.at[w, s], (to, c)
        )

    def height(w):
        return z if w == 1 else line - 1 - z

    def sends(w, s):
        return (height(w) <= s) & (height(w) < line - 1)

    def arrives(w, s):
        return (height(w) > 0) & (height(w) - 1 <= s)

    for s in range(line - 1):
        combine(order(s))
        if s > 0:
            for w in (1, 0):
                @pl.when(arrives(w, s - 1))
                def _():
                    zcopy(w, s - 1).wait_recv()
        for w in (1, 0):
            blk = z + (2 * w - 1) * (line - 1 - s)

            @pl.when(sends(w, s) & (height(w) > 0))
            def _():
                if s > 0:
                    out_stage[w, s] = (acc[blk] + line_in[w, s - 1].astype(F32)).astype(BF16)
                    zcopy(w, s).start()

            @pl.when(sends(w, s) & (height(w) == 0))
            def _():
                out_stage[w, s] = acc[blk].astype(BF16)
                zcopy(w, s).start()
    combine(z)
    final = line - 2
    for w in (1, 0):
        @pl.when(arrives(w, final))
        def _():
            zcopy(w, final).wait_recv()
            acc[z] = acc[z] + line_in[w, final].astype(F32)
    mixed_ref[...] = acc[z].astype(BF16)

    for b in range(experts):
        tcopy(b).wait_send()
    for zp in range(line):
        for r in range(3):
            xcopy(zp, r).wait_send()
    for s in range(line - 1):
        for w in (1, 0):
            @pl.when(sends(w, s))
            def _():
                zcopy(w, s).wait_send()


def vmem(count):
    return [pl.BlockSpec(memory_space=pltpu.VMEM)] * count


DMA = pltpu.SemaphoreType.DMA


def planar(pool, select, reward_w, routes, gates, target, w_gate, w_up, w_down):
    dp = lax.axis_size("dp")
    line = dp // PLANE
    experts = dp * w_gate.shape[0]
    sel_rows, top = routes.shape
    capacity = 5 * sel_rows * top // (4 * experts)
    pad = -(-capacity // 16) * 16
    half = target.shape[1]
    width = w_gate.shape[2]
    sel = (select - lax.axis_index("dp") * pool.shape[0]).reshape(sel_rows, 1)
    rw = jnp.broadcast_to(reward_w[None, :], (16, half))
    rows_shape = jax.ShapeDtypeStruct((experts, pad, width), BF16)
    tokens, cots, side = pl.pallas_call(
        functools.partial(dispatch_kernel, line, pad),
        name="dispatch",
        out_shape=(
            rows_shape, rows_shape, jax.ShapeDtypeStruct((line, 2 * experts, sel_rows), F32)
        ),
        in_specs=vmem(6),
        out_specs=tuple(vmem(3)),
        scratch_shapes=[
            pltpu.VMEM((2, line, sel_rows, half), BF16),
            pltpu.VMEM((line, experts, sel_rows), F32),
            pltpu.VMEM((16, sel_rows), F32),
            pltpu.VMEM((16, sel_rows), F32),
            pltpu.VMEM((2, line, 3, pad, half), BF16),
            DMA((2, 2, line)), DMA((2, line)), DMA((2, line)), DMA((line,)),
            DMA((2, line)), DMA((line,)), DMA((2, line, 3)), DMA((2, experts)),
            DMA((2, experts)), DMA((2, experts)), DMA, DMA,
        ],
        compiler_params=pltpu.CompilerParams(
            collective_id=0, has_side_effects=True, vmem_limit_bytes=50 * 2**20
        ),
    )(pool, sel, rw, routes.T, gates.T, target)
    token_rows = tokens.reshape(experts * pad, width)
    cot_rows = cots.reshape(experts * pad, width)
    wg, wu, wd = w_gate[0], w_up[0], w_down[0]
    dot = functools.partial(jnp.einsum, preferred_element_type=F32)
    gate_act = dot("rd,fd->rf", token_rows, wg)
    up_act = dot("rd,fd->rf", token_rows, wu)
    sig = jax.nn.sigmoid(gate_act)
    hidden = (gate_act * sig * up_act).astype(BF16)
    value = dot("rf,fd->rd", hidden, wd).astype(BF16).reshape(experts, pad, width)
    mixed = pl.pallas_call(
        functools.partial(return_kernel, line, pad),
        name="give_back",
        out_shape=jax.ShapeDtypeStruct((sel_rows, half), BF16),
        in_specs=vmem(2),
        out_specs=vmem(1)[0],
        scratch_shapes=[
            pltpu.VMEM((experts, pad, half), BF16),
            pltpu.VMEM((line, 3, pad, half), BF16),
            pltpu.VMEM((line, PLANE, pad, half), BF16),
            pltpu.VMEM((line, sel_rows, half), F32),
            pltpu.VMEM((2, line, sel_rows, half), BF16),
            pltpu.VMEM((2, line, sel_rows, half), BF16),
            DMA((experts,)), DMA((experts,)), DMA((line, 3)), DMA((line, PLANE)),
            DMA((2, line)), DMA((2, line)),
        ],
        compiler_params=pltpu.CompilerParams(
            collective_id=1, has_side_effects=True, vmem_limit_bytes=50 * 2**20
        ),
    )(value, side)
    hidden_grad = dot("rd,fd->rf", cot_rows, wd)
    gate_grad = (hidden_grad * up_act * sig * (1.0 + gate_act * (1.0 - sig))).astype(BF16)
    up_grad = (hidden_grad * gate_act * sig).astype(BF16)
    grad_down = dot("rf,rd->fd", hidden, cot_rows).astype(BF16)[None]
    grad_gate = dot("rf,rd->fd", gate_grad, token_rows).astype(BF16)[None]
    grad_up = dot("rf,rd->fd", up_grad, token_rows).astype(BF16)[None]
    return mixed, grad_gate, grad_up, grad_down


def solution(mesh):
    in_specs = (
        P("dp", "tensor"), P("dp"), P("tensor"), P("dp", None), P("dp", None), P("dp", "tensor"),
        P("dp", "tensor", None), P("dp", "tensor", None), P("dp", "tensor", None),
    )
    out_specs = (
        P("dp", "tensor"), P("dp", "tensor", None), P("dp", "tensor", None),
        P("dp", "tensor", None),
    )
    dp, tensor = mesh.shape["dp"], mesh.shape["tensor"]
    fits = tensor == 2 and dp % (2 * PLANE) == 0
    local = planar if fits else generic
    return jax.shard_map(local, mesh=mesh, in_specs=in_specs, out_specs=out_specs, check_vma=False)
```

```python
import functools
import jax
import jax.numpy as jnp
from jax import lax
from jax.experimental import pallas as pl
from jax.experimental.pallas import tpu as pltpu
from jax.sharding import PartitionSpec as P

MESH = pl.DeviceIdType.MESH
PLANE = 4
F32 = jnp.float32
BF16 = jnp.bfloat16


def slot_factor(route_hit, weights):
    return jnp.sum(jnp.where(route_hit, weights.reshape(-1)[:, None], 0.0), axis=0)


def generic(pool, select, reward_w, routes, gates, target, w_gate, w_up, w_down):
    pool_rows = pool.shape[0]
    local_rows = select - lax.axis_index("dp") * pool_rows
    chosen = jnp.take(pool, local_rows, axis=0)
    sel_rows, top_count = routes.shape
    owners = lax.axis_size("dp")
    exp_dev = w_gate.shape[0]
    experts = owners * exp_dev
    capacity = 5 * sel_rows * top_count // (4 * experts)
    slot_count = experts * capacity
    flat_routes = routes.reshape(-1)
    onehot = (flat_routes[:, None] == jnp.arange(experts, dtype=jnp.int32)[None, :]).astype(
        jnp.int32
    )
    before = jnp.cumsum(onehot, axis=0) - onehot
    slot_rank = jnp.sum(before * onehot, axis=1)
    slot_place = flat_routes * capacity + slot_rank
    route_hit = slot_place[:, None] == jnp.arange(slot_count, dtype=jnp.int32)[None, :]
    route_pick = route_hit.astype(jnp.bfloat16).reshape(sel_rows, top_count, slot_count)
    token_pick = jnp.sum(route_pick, axis=1)
    reward = lax.psum(jnp.dot(chosen, reward_w, preferred_element_type=jnp.float32), "tensor")
    keep_scale = jax.nn.sigmoid(reward)
    slot_scale = slot_factor(route_hit, keep_scale[:, None] * gates)
    token_send = jnp.einsum(
        "sp,sd->pd", token_pick, chosen, preferred_element_type=jnp.float32
    ).astype(jnp.bfloat16)
    picked_target = jnp.einsum("sp,sd->pd", token_pick, target, preferred_element_type=jnp.float32)
    cot_send = (picked_target * slot_scale[:, None]).astype(jnp.bfloat16)
    token_part, cot_part = (
        lax.all_to_all(token_send, "dp", split_axis=0, concat_axis=0, tiled=True),
        lax.all_to_all(cot_send, "dp", split_axis=0, concat_axis=0, tiled=True),
    )
    received_tokens, received_cots = (
        lax.all_gather(token_part, "tensor", axis=1, tiled=True),
        lax.all_gather(cot_part, "tensor", axis=1, tiled=True),
    )
    width = received_tokens.shape[1]
    token_rows = received_tokens.reshape(owners, exp_dev, capacity, width)
    cot_rows = received_cots.reshape(owners, exp_dev, capacity, width)
    gate_act = jnp.einsum("secd,efd->secf", token_rows, w_gate, preferred_element_type=jnp.float32)
    up_act = jnp.einsum("secd,efd->secf", token_rows, w_up, preferred_element_type=jnp.float32)
    sigmoid_gate = jax.nn.sigmoid(gate_act)
    hidden = (gate_act * sigmoid_gate * up_act).astype(jnp.bfloat16)
    partial_value = jnp.einsum("secf,efd->secd", hidden, w_down, preferred_element_type=jnp.float32)
    summed = lax.psum_scatter(
        partial_value.astype(jnp.bfloat16), "tensor", scatter_dimension=3, tiled=True
    )
    returned = lax.all_to_all(summed, "dp", split_axis=0, concat_axis=0, tiled=True).reshape(
        slot_count, -1
    )
    route_rows = jnp.einsum("skp,pd->skd", route_pick, returned, preferred_element_type=jnp.float32)
    mixed = jnp.sum(route_rows * gates[:, :, None], axis=1).astype(jnp.bfloat16)
    hidden_grad = jnp.einsum("secd,efd->secf", cot_rows, w_down, preferred_element_type=jnp.float32)
    gate_grad = (
        hidden_grad * up_act * sigmoid_gate * (1.0 + gate_act * (1.0 - sigmoid_gate))
    ).astype(jnp.bfloat16)
    up_grad = (hidden_grad * gate_act * sigmoid_gate).astype(jnp.bfloat16)
    grad_down = jnp.einsum(
        "secf,secd->efd", hidden, cot_rows, preferred_element_type=jnp.float32
    ).astype(jnp.bfloat16)
    grad_gate = jnp.einsum(
        "secf,secd->efd", gate_grad, token_rows, preferred_element_type=jnp.float32
    ).astype(jnp.bfloat16)
    grad_up = jnp.einsum(
        "secf,secd->efd", up_grad, token_rows, preferred_element_type=jnp.float32
    ).astype(jnp.bfloat16)
    return (mixed, grad_gate, grad_up, grad_down)


def place(line):
    d = lax.axis_index("dp")
    c = lax.axis_index("tensor")
    z, q = d // PLANE, d % PLANE
    y, x = q // 2, q % 2
    mates = [((y + ry) % 2) * 2 + (x + rx) % 2 for ry, rx in ((0, 1), (1, 0), (1, 1))]
    return d, c, z, q, mates


def greet(d, c, z, q, mates, line):
    barrier = pltpu.get_barrier_semaphore()
    for m in mates:
        pl.semaphore_signal(barrier, inc=1, device_id=(z * PLANE + m, c), device_id_type=MESH)
    pl.semaphore_signal(barrier, inc=1, device_id=(d, 1 - c), device_id_type=MESH)

    @pl.when(z > 0)
    def _():
        pl.semaphore_signal(barrier, inc=1, device_id=(d - PLANE, c), device_id_type=MESH)

    @pl.when(z < line - 1)
    def _():
        pl.semaphore_signal(barrier, inc=1, device_id=(d + PLANE, c), device_id_type=MESH)

    below, above = (z + line - 1) // line, (2 * line - 2 - z) // line
    pl.semaphore_wait(barrier, 4 + below + above)


def remote(src, dst, send, recv, dev):
    return pltpu.make_async_remote_copy(
        src_ref=src, dst_ref=dst, send_sem=send, recv_sem=recv, device_id=dev, device_id_type=MESH
    )


def layer_kernel(
    line, pad, pool_hbm, sel_ref, rw_ref, rt_ref, gt_ref, target_hbm, wg_hbm, wu_hbm, wd_hbm,
    mixed_ref, gg_hbm, gu_hbm, gd_hbm,
    pool_ref, wide, wg, wu, wd, tok, cot, gate_act, up_act, hid, ggrad, ugrad, val,
    data, side_ref, scale, part, part_in, stage,
    partner_in, back, plane_in, acc, out_stage, line_in,
    lsem, osem, zsend, zrecv, ssend, srecv, csend, crecv, xsend, xrecv, tsend, trecv, psend, precv,
    vsend, vrecv, bsend, brecv, usend, urecv,
):
    d, c, z, q, mates = place(line)
    experts = line * PLANE
    sel_rows, half = mixed_ref.shape
    top = gt_ref.shape[1]
    units, width = wg.shape
    span = PLANE * pad
    rows = (tok, cot)
    mine = pl.ds(pl.multiple_of(c * half, half), half)
    other = pl.ds(pl.multiple_of((1 - c) * half, half), half)
    partner = (d, 1 - c)
    turn = 2 * (z // (line // 2)) - 1

    def order(i):
        return (z + turn * (1 + i) + 2 * line) % line

    loads = [
        pltpu.make_async_copy(src, dst, lsem.at[i])
        for i, (src, dst) in enumerate((
            (pool_hbm, pool_ref), (target_hbm, data.at[1, z]), (wg_hbm.at[0], wg),
            (wu_hbm.at[0], wu), (wd_hbm.at[0], wd),
        ))
    ]
    for cp in loads:
        cp.start()

    wide[0, :, 0:top] = rt_ref[...].astype(F32)
    wide[1, :, 0:top] = gt_ref[...]
    routes_t = wide[0].T
    gates_t = wide[1].T
    expert_id = lax.broadcasted_iota(jnp.int32, (experts, sel_rows), 0).astype(F32)
    member = jnp.zeros((experts, sel_rows), F32)
    gate = jnp.zeros((experts, sel_rows), F32)
    for k in range(top):
        eq = routes_t[k : k + 1, :] == expert_id
        member = member + jnp.where(eq, 1.0, 0.0)
        gate = gate + jnp.where(eq, gates_t[k : k + 1, :], 0.0)
    tri = jnp.where(
        lax.broadcasted_iota(jnp.int32, (sel_rows, sel_rows), 0)
        < lax.broadcasted_iota(jnp.int32, (sel_rows, sel_rows), 1),
        1.0,
        0.0,
    ).astype(BF16)
    before = jnp.dot(member.astype(BF16), tri, preferred_element_type=F32)
    side_ref[z, 0:experts, :] = jnp.where(member > 0.5, before, -1.0)
    side_ref[z, experts : 2 * experts, :] = gate

    pool_rows = pool_ref.shape[0]
    hit = (
        lax.broadcasted_iota(jnp.int32, (pool_rows, sel_rows), 0) == sel_ref[...] - d * pool_rows
    ).astype(F32).astype(BF16)
    loads[0].wait()
    chosen = lax.dot_general(
        hit, pool_ref[...], (((0,), (0,)), ((), ())), preferred_element_type=F32
    ).astype(BF16)
    data[0, z] = chosen
    part[...] = lax.dot_general(
        jnp.broadcast_to(rw_ref[...].astype(F32), (16, half)).astype(BF16), chosen,
        (((1,), (1,)), ((), ())), preferred_element_type=F32,
    )

    greet(d, c, z, q, mates, line)
    reward_copy = remote(part, part_in, psend, precv, partner)
    reward_copy.start()

    def zcopies(a, s, way):
        blk = z - way * s
        dev = (d + way * PLANE, c)
        w = (way + 1) // 2
        main = remote(data.at[a, blk], data.at[a, blk], zsend.at[a, w, s], zrecv.at[a, blk], dev)
        if a == 0:
            extra = remote(
                side_ref.at[blk], side_ref.at[blk], ssend.at[w, s], srecv.at[blk], dev
            )
        else:
            extra = remote(scale.at[blk], scale.at[blk], csend.at[w, s], crecv.at[blk], dev)
        return extra, main

    def sends(a, s, way):
        blk, to = z - way * s, z + way
        return (blk >= 0) & (blk < line) & (to >= 0) & (to < line)

    def zstart(a, s):
        for way in (1, -1):
            @pl.when(sends(a, s, way))
            def _():
                for cp in zcopies(a, s, way):
                    cp.start()

    def arrives(s, way):
        blk = z - way * (s + 1)
        return (blk >= 0) & (blk < line)

    def zwait(a, s):
        for way in (1, -1):
            @pl.when(arrives(s, way))
            def _():
                blk = z - way * (s + 1)
                remote(
                    data.at[a, blk], data.at[a, blk], zsend.at[a, 0, 0], zrecv.at[a, blk], partner
                ).wait_recv()
                if a == 0:
                    remote(
                        side_ref.at[blk], side_ref.at[blk], ssend.at[0, 0], srecv.at[blk], partner
                    ).wait_recv()
                else:
                    remote(
                        scale.at[blk], scale.at[blk], csend.at[0, 0], crecv.at[blk], partner
                    ).wait_recv()

    def tcopy(a, b):
        spot = rows[a].at[b, :, mine]
        return remote(spot, spot, tsend.at[a, b], trecv.at[a, b], partner)

    def tarrive(a, b):
        spot = rows[a].at[b, :, other]
        remote(spot, spot, tsend.at[a, b], trecv.at[a, b], partner).wait_recv()

    def xcopy(a, zp, r):
        return remote(
            stage.at[a, zp, r],
            rows[a].at[zp * PLANE + q, :, mine],
            xsend.at[a, zp, r],
            xrecv.at[a, zp * PLANE + q],
            (z * PLANE + mates[r], c),
        )

    slot_id = lax.broadcasted_iota(jnp.int32, (pad, sel_rows), 0).astype(F32)

    def process(a, zp):
        block = data[a, zp]
        for r in (2, 0, 1, 3):
            e = z * PLANE + (mates[r] if r < 3 else q)
            m = slot_id == side_ref[zp, pl.ds(e, 1), :]
            picked = jnp.dot(
                jnp.where(m, 1.0, 0.0).astype(BF16), block, preferred_element_type=F32
            )
            if a == 1:
                picked = picked * jnp.sum(
                    jnp.where(m, scale[zp, pl.ds(e, 1), :], 0.0), axis=1, keepdims=True
                )
            picked = picked.astype(BF16)
            if r < 3:
                stage[a, zp, r] = picked
                xcopy(a, zp, r).start()
            else:
                rows[a][zp * PLANE + q, :, mine] = picked
                tcopy(a, zp * PLANE + q).start()

    def forward(a, zp):
        for r in range(3):
            b = zp * PLANE + mates[r]
            remote(
                stage.at[a, zp, r], rows[a].at[b, :, mine], xsend.at[a, zp, r],
                xrecv.at[a, b], partner,
            ).wait_recv()
            tcopy(a, b).start()

    def got(fn, a, s):
        for way in (1, -1):
            @pl.when(arrives(s, way))
            def _():
                fn(a, z - way * (s + 1))

    def vcopy(b):
        return remote(val.at[b, :, other], partner_in.at[b], vsend.at[b], vrecv.at[b], partner)

    def lanes(zp):
        return pl.ds(pl.multiple_of(zp * span, span), span)

    def sigmoid(v):
        return 1.0 / (1.0 + jnp.exp(-v))

    nt = (((1,), (1,)), ((), ()))
    tn = (((0,), (0,)), ((), ()))
    tile = 512 if width % 512 == 0 else width

    def group(zp):
        for j in range(PLANE):
            tarrive(0, zp * PLANE + j)
        x = tok[pl.ds(zp * PLANE, PLANE)].reshape(span, width)
        g = lax.dot_general(wg[...], x, nt, preferred_element_type=F32)
        u = lax.dot_general(wu[...], x, nt, preferred_element_type=F32)
        gate_act[zp] = g
        up_act[zp] = u
        h = (g * sigmoid(g) * u).astype(BF16)
        hid[:, lanes(zp)] = h
        for n in range(width // tile):
            cols = pl.ds(n * tile, tile)
            v = lax.dot_general(h, wd[:, cols], tn, preferred_element_type=F32)
            val[pl.ds(zp * PLANE, PLANE), :, cols] = v.astype(BF16).reshape(PLANE, pad, tile)
        for j in range(PLANE):
            vcopy(zp * PLANE + j).start()

    def grad_group(zp):
        for j in range(PLANE):
            tarrive(1, zp * PLANE + j)
        x = cot[pl.ds(zp * PLANE, PLANE)].reshape(span, width)
        hg = lax.dot_general(wd[...], x, nt, preferred_element_type=F32)
        g = gate_act[zp]
        s = sigmoid(g)
        ggrad[:, lanes(zp)] = (hg * up_act[zp] * s * (1.0 + g * (1.0 - s))).astype(BF16)
        ugrad[:, lanes(zp)] = (hg * g * s).astype(BF16)

    grads = ((ggrad, tok, wg, gg_hbm), (ugrad, tok, wu, gu_hbm), (hid, cot, wd, gd_hbm))
    strip = 256 if width % 256 == 0 else width
    strips = width // strip

    def ocopy(g, n):
        cols = pl.ds(pl.multiple_of(n * strip, strip), strip)
        return pltpu.make_async_copy(
            grads[g][2].at[:, cols], grads[g][3].at[0, :, cols], osem.at[g, n]
        )

    def grad_strip(n, carry):
        cols = pl.ds(pl.multiple_of(n * strip, strip), strip)
        for g, (left, right, out, _) in enumerate(grads):
            r = right[:, :, cols].reshape(experts * pad, strip)
            out[:, cols] = jnp.dot(left[...], r, preferred_element_type=F32).astype(BF16)
            ocopy(g, n).start()
        return carry

    def bcopy(zp, r):
        return remote(
            back.at[zp, r], plane_in.at[zp, q], bsend.at[zp, r], brecv.at[zp, q],
            (z * PLANE + mates[r], c),
        )

    def give(zp):
        for r in (2, 0, 1, 3):
            b = zp * PLANE + (mates[r] if r < 3 else q)
            vcopy(b).wait_recv()
            total = (val[b, :, mine].astype(F32) + partner_in[b].astype(F32)).astype(BF16)
            if r < 3:
                back[zp, r] = total
                bcopy(zp, r).start()
            else:
                plane_in[zp, q] = total

    def combine(zp):
        for r in range(3):
            remote(
                back.at[zp, r], plane_in.at[zp, mates[r]], bsend.at[zp, r],
                brecv.at[zp, mates[r]], partner,
            ).wait_recv()
        total = jnp.zeros((sel_rows, half), F32)
        for j in range(PLANE):
            e = z * PLANE + j
            w = jnp.where(
                slot_id == side_ref[zp, pl.ds(e, 1), :],
                side_ref[zp, pl.ds(experts + e, 1), :],
                0.0,
            )
            high = w.astype(BF16)
            low = (w - high.astype(F32)).astype(BF16)
            both = jnp.concatenate([high, low], axis=0)
            values = plane_in[zp, j]
            total = total + lax.dot_general(
                both, jnp.concatenate([values, values], axis=0), tn, preferred_element_type=F32
            )
        acc[zp] = total

    def ucopy(w, s):
        to = d + (2 * w - 1) * PLANE
        return remote(
            out_stage.at[w, s], line_in.at[w, s], usend.at[w, s], urecv.at[w, s], (to, c)
        )

    def height(w):
        return z if w == 1 else line - 1 - z

    def lifts(w, s):
        return (height(w) <= s) & (height(w) < line - 1)

    def lands(w, s):
        return (height(w) > 0) & (height(w) - 1 <= s)

    zstart(0, 0)
    process(0, z)
    reward_copy.wait()
    scale[z] = sigmoid(part[0:1, :] + part_in[0:1, :]) * side_ref[z, experts : 2 * experts, :]
    last = line - 2
    for a in (0, 1):
        for s in range(line - 1):
            zwait(a, s)
            if s < last:
                zstart(a, s + 1)
            elif a == 0:
                loads[1].wait()
                zstart(1, 0)
            got(process, a, s)
            if s == 0:
                forward(a, z)
            else:
                got(forward, a, s - 1)
            if a == 1:
                if s == last:
                    for i in range(line - 1):
                        give(order(i))
                    group(order(line - 1))
                else:
                    group(order(s + 1))
        if a == 0:
            process(1, z)
        got(forward, a, last)
        if a == 0:
            for cp in loads[2:]:
                cp.wait()
            group(order(0))
    give(z)

    for i in range(line):
        grad_group(order(line - 1 - i))
    done = 0
    for s in range(line - 1):
        combine(order(s))
        if s > 0:
            for w in (1, 0):
                @pl.when(lands(w, s - 1))
                def _():
                    ucopy(w, s - 1).wait_recv()
        for w in (1, 0):
            blk = z + (2 * w - 1) * (line - 1 - s)

            @pl.when(lifts(w, s) & (height(w) > 0))
            def _():
                if s > 0:
                    out_stage[w, s] = (acc[blk] + line_in[w, s - 1].astype(F32)).astype(BF16)
                    ucopy(w, s).start()

            @pl.when(lifts(w, s) & (height(w) == 0))
            def _():
                out_stage[w, s] = acc[blk].astype(BF16)
                ucopy(w, s).start()
        upto = strips * (s + 1) // line
        lax.fori_loop(done, upto, grad_strip, 0)
        done = upto
    combine(z)
    lax.fori_loop(done, strips, grad_strip, 0)
    for w in (1, 0):
        @pl.when(lands(w, last))
        def _():
            ucopy(w, last).wait_recv()
            acc[z] = acc[z] + line_in[w, last].astype(F32)
    mixed_ref[...] = acc[z].astype(BF16)

    for g in range(3):
        for n in range(strips):
            ocopy(g, n).wait()
    for b in range(experts):
        vcopy(b).wait_send()
        for a in (0, 1):
            tcopy(a, b).wait_send()
    for zp in range(line):
        for r in range(3):
            bcopy(zp, r).wait_send()
            for a in (0, 1):
                xcopy(a, zp, r).wait_send()
    for s in range(line - 1):
        for w in (1, 0):
            @pl.when(lifts(w, s))
            def _():
                ucopy(w, s).wait_send()

        for a in (0, 1):
            for way in (1, -1):
                @pl.when(sends(a, s, way))
                def _():
                    for cp in zcopies(a, s, way):
                        cp.wait_send()


def vmem(count):
    return [pl.BlockSpec(memory_space=pltpu.VMEM)] * count


def hbm(count):
    return [pl.BlockSpec(memory_space=pl.ANY)] * count


DMA = pltpu.SemaphoreType.DMA


def planar(pool, select, reward_w, routes, gates, target, w_gate, w_up, w_down):
    dp = lax.axis_size("dp")
    line = dp // PLANE
    experts = dp * w_gate.shape[0]
    sel_rows, top = routes.shape
    capacity = 5 * sel_rows * top // (4 * experts)
    pad = -(-capacity // 16) * 16
    half = target.shape[1]
    units, width = w_gate.shape[1:]
    span = PLANE * pad
    grad_shape = jax.ShapeDtypeStruct(w_gate.shape, BF16)
    mat = pltpu.VMEM((units, width), BF16)
    slots = pltpu.VMEM((experts, pad, width), BF16)
    act = pltpu.VMEM((line, units, span), F32)
    flat = pltpu.VMEM((units, experts * pad), BF16)
    return pl.pallas_call(
        functools.partial(layer_kernel, line, pad),
        name="layer",
        out_shape=(jax.ShapeDtypeStruct((sel_rows, half), BF16), grad_shape, grad_shape, grad_shape),
        in_specs=hbm(1) + vmem(4) + hbm(4),
        out_specs=tuple(vmem(1) + hbm(3)),
        scratch_shapes=[
            pltpu.VMEM(pool.shape, BF16), pltpu.VMEM((2, sel_rows, sel_rows), F32),
            mat, mat, mat, slots, slots, act, act, flat, flat, flat, slots,
            pltpu.VMEM((2, line, sel_rows, half), BF16),
            pltpu.VMEM((line, 2 * experts, sel_rows), F32),
            pltpu.VMEM((line, experts, sel_rows), F32),
            pltpu.VMEM((16, sel_rows), F32),
            pltpu.VMEM((16, sel_rows), F32),
            pltpu.VMEM((2, line, 3, pad, half), BF16),
            pltpu.VMEM((experts, pad, half), BF16),
            pltpu.VMEM((line, 3, pad, half), BF16),
            pltpu.VMEM((line, PLANE, pad, half), BF16),
            pltpu.VMEM((line, sel_rows, half), F32),
            pltpu.VMEM((2, line - 1, sel_rows, half), BF16),
            pltpu.VMEM((2, line - 1, sel_rows, half), BF16),
            DMA((5,)), DMA((3, width // 256)),
            DMA((2, 2, line)), DMA((2, line)), DMA((2, line)), DMA((line,)),
            DMA((2, line)), DMA((line,)), DMA((2, line, 3)), DMA((2, experts)),
            DMA((2, experts)), DMA((2, experts)), DMA, DMA,
            DMA((experts,)), DMA((experts,)), DMA((line, 3)), DMA((line, PLANE)),
            DMA((2, line)), DMA((2, line)),
        ],
        compiler_params=pltpu.CompilerParams(
            collective_id=0, has_side_effects=True, vmem_limit_bytes=67043328
        ),
    )(pool, select.reshape(1, sel_rows), reward_w.reshape(1, half), routes, gates, target,
      w_gate, w_up, w_down)


def solution(mesh):
    in_specs = (
        P("dp", "tensor"), P("dp"), P("tensor"), P("dp", None), P("dp", None), P("dp", "tensor"),
        P("dp", "tensor", None), P("dp", "tensor", None), P("dp", "tensor", None),
    )
    out_specs = (
        P("dp", "tensor"), P("dp", "tensor", None), P("dp", "tensor", None),
        P("dp", "tensor", None),
    )
    dp, tensor = mesh.shape["dp"], mesh.shape["tensor"]
    fits = tensor == 2 and dp % (2 * PLANE) == 0
    local = planar if fits else generic
    return jax.shard_map(local, mesh=mesh, in_specs=in_specs, out_specs=out_specs, check_vma=False)
```

```python
import functools
import jax
import jax.numpy as jnp
from jax import lax
from jax.experimental import pallas as pl
from jax.experimental.pallas import tpu as pltpu
from jax.sharding import PartitionSpec as P

MESH = pl.DeviceIdType.MESH
PLANE = 4
F32 = jnp.float32
BF16 = jnp.bfloat16


def slot_factor(route_hit, weights):
    return jnp.sum(jnp.where(route_hit, weights.reshape(-1)[:, None], 0.0), axis=0)


def generic(pool, select, reward_w, routes, gates, target, w_gate, w_up, w_down):
    pool_rows = pool.shape[0]
    local_rows = select - lax.axis_index("dp") * pool_rows
    chosen = jnp.take(pool, local_rows, axis=0)
    sel_rows, top_count = routes.shape
    owners = lax.axis_size("dp")
    exp_dev = w_gate.shape[0]
    experts = owners * exp_dev
    capacity = 5 * sel_rows * top_count // (4 * experts)
    slot_count = experts * capacity
    flat_routes = routes.reshape(-1)
    onehot = (flat_routes[:, None] == jnp.arange(experts, dtype=jnp.int32)[None, :]).astype(
        jnp.int32
    )
    before = jnp.cumsum(onehot, axis=0) - onehot
    slot_rank = jnp.sum(before * onehot, axis=1)
    slot_place = flat_routes * capacity + slot_rank
    route_hit = slot_place[:, None] == jnp.arange(slot_count, dtype=jnp.int32)[None, :]
    route_pick = route_hit.astype(jnp.bfloat16).reshape(sel_rows, top_count, slot_count)
    token_pick = jnp.sum(route_pick, axis=1)
    reward = lax.psum(jnp.dot(chosen, reward_w, preferred_element_type=jnp.float32), "tensor")
    keep_scale = jax.nn.sigmoid(reward)
    slot_scale = slot_factor(route_hit, keep_scale[:, None] * gates)
    token_send = jnp.einsum(
        "sp,sd->pd", token_pick, chosen, preferred_element_type=jnp.float32
    ).astype(jnp.bfloat16)
    picked_target = jnp.einsum("sp,sd->pd", token_pick, target, preferred_element_type=jnp.float32)
    cot_send = (picked_target * slot_scale[:, None]).astype(jnp.bfloat16)
    token_part, cot_part = (
        lax.all_to_all(token_send, "dp", split_axis=0, concat_axis=0, tiled=True),
        lax.all_to_all(cot_send, "dp", split_axis=0, concat_axis=0, tiled=True),
    )
    received_tokens, received_cots = (
        lax.all_gather(token_part, "tensor", axis=1, tiled=True),
        lax.all_gather(cot_part, "tensor", axis=1, tiled=True),
    )
    width = received_tokens.shape[1]
    token_rows = received_tokens.reshape(owners, exp_dev, capacity, width)
    cot_rows = received_cots.reshape(owners, exp_dev, capacity, width)
    gate_act = jnp.einsum("secd,efd->secf", token_rows, w_gate, preferred_element_type=jnp.float32)
    up_act = jnp.einsum("secd,efd->secf", token_rows, w_up, preferred_element_type=jnp.float32)
    sigmoid_gate = jax.nn.sigmoid(gate_act)
    hidden = (gate_act * sigmoid_gate * up_act).astype(jnp.bfloat16)
    partial_value = jnp.einsum("secf,efd->secd", hidden, w_down, preferred_element_type=jnp.float32)
    summed = lax.psum_scatter(
        partial_value.astype(jnp.bfloat16), "tensor", scatter_dimension=3, tiled=True
    )
    returned = lax.all_to_all(summed, "dp", split_axis=0, concat_axis=0, tiled=True).reshape(
        slot_count, -1
    )
    route_rows = jnp.einsum("skp,pd->skd", route_pick, returned, preferred_element_type=jnp.float32)
    mixed = jnp.sum(route_rows * gates[:, :, None], axis=1).astype(jnp.bfloat16)
    hidden_grad = jnp.einsum("secd,efd->secf", cot_rows, w_down, preferred_element_type=jnp.float32)
    gate_grad = (
        hidden_grad * up_act * sigmoid_gate * (1.0 + gate_act * (1.0 - sigmoid_gate))
    ).astype(jnp.bfloat16)
    up_grad = (hidden_grad * gate_act * sigmoid_gate).astype(jnp.bfloat16)
    grad_down = jnp.einsum(
        "secf,secd->efd", hidden, cot_rows, preferred_element_type=jnp.float32
    ).astype(jnp.bfloat16)
    grad_gate = jnp.einsum(
        "secf,secd->efd", gate_grad, token_rows, preferred_element_type=jnp.float32
    ).astype(jnp.bfloat16)
    grad_up = jnp.einsum(
        "secf,secd->efd", up_grad, token_rows, preferred_element_type=jnp.float32
    ).astype(jnp.bfloat16)
    return (mixed, grad_gate, grad_up, grad_down)


def place(line):
    d = lax.axis_index("dp")
    c = lax.axis_index("tensor")
    z, q = d // PLANE, d % PLANE
    y, x = q // 2, q % 2
    mates = [((y + ry) % 2) * 2 + (x + rx) % 2 for ry, rx in ((0, 1), (1, 0), (1, 1))]
    return d, c, z, q, mates


def greet(d, c, z, q, mates, line):
    barrier = pltpu.get_barrier_semaphore()
    for m in mates:
        pl.semaphore_signal(barrier, inc=1, device_id=(z * PLANE + m, c), device_id_type=MESH)
    pl.semaphore_signal(barrier, inc=1, device_id=(d, 1 - c), device_id_type=MESH)

    for k in range(1, line):
        pl.semaphore_signal(
            barrier, inc=1, device_id=((z + k) % line * PLANE + q, c), device_id_type=MESH
        )


def greeted(line):
    pl.semaphore_wait(pltpu.get_barrier_semaphore(), PLANE + line - 1)


def remote(src, dst, send, recv, dev):
    return pltpu.make_async_remote_copy(
        src_ref=src, dst_ref=dst, send_sem=send, recv_sem=recv, device_id=dev, device_id_type=MESH
    )


def layer_kernel(
    line, pad, pool_hbm, sel_ref, rw_ref, rt_ref, gt_ref, target_hbm, wg_hbm, wu_hbm, wd_hbm,
    mixed_ref, gg_ref, gu_ref, gd_ref,
    pool_ref, rt_vmem, gt_vmem, tok, cot, gate_act, up_act, hid, ggrad, ugrad, val,
    data, side_ref, scale, part, part_in, stage,
    partner_in, back, plane_in, acc, out_stage, line_in,
    lsem, zsend, zrecv, ssend, srecv, csend, crecv, xsend, xrecv, tsend, trecv, psend, precv,
    vsend, vrecv, bsend, brecv, usend, urecv,
):
    d, c, z, q, mates = place(line)
    experts = line * PLANE
    sel_rows, half = mixed_ref.shape
    top = gt_ref.shape[0]
    wg, wu, wd = gg_ref.at[0], gu_ref.at[0], gd_ref.at[0]
    units, width = wg.shape
    span = PLANE * pad
    rows = (tok, cot)
    mine = pl.ds(pl.multiple_of(c * half, half), half)
    other = pl.ds(pl.multiple_of((1 - c) * half, half), half)
    partner = (d, 1 - c)
    turn = 2 * (z // (line // 2)) - 1

    def order(i):
        return (z + turn * (1 + i) + 2 * line) % line

    greet(d, c, z, q, mates, line)
    loads = [
        pltpu.make_async_copy(src, dst, lsem.at[i])
        for i, (src, dst) in enumerate((
            (pool_hbm, pool_ref), (target_hbm, data.at[1, z]), (wg_hbm.at[0], wg),
            (wu_hbm.at[0], wu), (wd_hbm.at[0], wd), (rt_ref, rt_vmem), (gt_ref, gt_vmem),
        ))
    ]
    for i in (5, 6, 0, 1, 2, 3, 4):
        loads[i].start()

    loads[5].wait()
    loads[6].wait()
    expert_id = lax.broadcasted_iota(jnp.int32, (experts, sel_rows), 0)
    member = jnp.zeros((experts, sel_rows), F32)
    gate = jnp.zeros((experts, sel_rows), F32)
    for k in range(top):
        eq = rt_vmem[k : k + 1, :] == expert_id
        member = member + jnp.where(eq, 1.0, 0.0)
        gate = gate + jnp.where(eq, gt_vmem[k : k + 1, :], 0.0)
    tri = jnp.where(
        lax.broadcasted_iota(jnp.int32, (sel_rows, sel_rows), 0)
        < lax.broadcasted_iota(jnp.int32, (sel_rows, sel_rows), 1),
        1.0,
        0.0,
    ).astype(BF16)
    before = jnp.dot(member.astype(BF16), tri, preferred_element_type=F32)
    side_ref[z, 0:experts, :] = jnp.where(member > 0.5, before, -1.0)
    side_ref[z, experts : 2 * experts, :] = gate

    pool_rows = pool_ref.shape[0]
    hit = (
        lax.broadcasted_iota(jnp.int32, (pool_rows, sel_rows), 0) == sel_ref[...] - d * pool_rows
    ).astype(F32).astype(BF16)
    loads[0].wait()
    chosen = lax.dot_general(
        hit, pool_ref[...], (((0,), (0,)), ((), ())), preferred_element_type=F32
    ).astype(BF16)
    data[0, z] = chosen
    part[...] = lax.dot_general(
        rw_ref[...], chosen,
        (((1,), (1,)), ((), ())), preferred_element_type=F32,
    )

    greeted(line)
    reward_copy = remote(part, part_in, psend, precv, partner)
    reward_copy.start()

    def zcopies(a, s, way):
        blk = z - way * s
        dev = (d + way * PLANE, c)
        w = (way + 1) // 2
        return (
            remote(side_ref.at[blk], side_ref.at[blk], ssend.at[w, s], srecv.at[blk], dev),
            remote(data.at[0, blk], data.at[0, blk], zsend.at[0, w, s], zrecv.at[0, blk], dev),
        )

    def sends(a, s, way):
        blk, to = z - way * s, z + way
        return (blk >= 0) & (blk < line) & (to >= 0) & (to < line)

    def lcopy(k, way):
        w = (way + 1) // 2
        dev = (d + way * k * PLANE, c)
        return (
            remote(scale.at[z], scale.at[z], csend.at[w, k], crecv.at[z], dev),
            remote(data.at[1, z], data.at[1, z], zsend.at[1, w, k], zrecv.at[1, z], dev),
        )

    def reaches(k, way):
        to = z + way * k
        return (to >= 0) & (to < line)

    def lstart():
        for k in range(1, line):
            for way in (1, -1):
                @pl.when(reaches(k, way))
                def _():
                    for cp in lcopy(k, way):
                        cp.start()

    def zstart(a, s):
        for way in (1, -1):
            @pl.when(sends(a, s, way))
            def _():
                for cp in zcopies(a, s, way):
                    cp.start()

    def arrives(s, way):
        blk = z - way * (s + 1)
        return (blk >= 0) & (blk < line)

    def zwait(a, s):
        for way in (1, -1):
            @pl.when(arrives(s, way))
            def _():
                blk = z - way * (s + 1)
                remote(
                    data.at[a, blk], data.at[a, blk], zsend.at[a, 0, 0], zrecv.at[a, blk], partner
                ).wait_recv()
                if a == 0:
                    remote(
                        side_ref.at[blk], side_ref.at[blk], ssend.at[0, 0], srecv.at[blk], partner
                    ).wait_recv()
                else:
                    remote(
                        scale.at[blk], scale.at[blk], csend.at[0, 0], crecv.at[blk], partner
                    ).wait_recv()

    def tcopy(a, b):
        spot = rows[a].at[b, :, mine]
        return remote(spot, spot, tsend.at[a, b], trecv.at[a, b], partner)

    def tarrive(a, b):
        spot = rows[a].at[b, :, other]
        remote(spot, spot, tsend.at[a, b], trecv.at[a, b], partner).wait_recv()

    def xcopy(a, zp, r):
        return remote(
            stage.at[a, zp, r],
            rows[a].at[zp * PLANE + q, :, mine],
            xsend.at[a, zp, r],
            xrecv.at[a, zp * PLANE + q],
            (z * PLANE + mates[r], c),
        )

    slot_id = lax.broadcasted_iota(jnp.int32, (pad, sel_rows), 0).astype(F32)

    def process(a, zp):
        block = data[a, zp]
        for r in (2, 0, 1, 3):
            e = z * PLANE + (mates[r] if r < 3 else q)
            m = slot_id == side_ref[zp, pl.ds(e, 1), :]
            picked = jnp.dot(
                jnp.where(m, 1.0, 0.0).astype(BF16), block, preferred_element_type=F32
            )
            if a == 1:
                picked = picked * jnp.sum(
                    jnp.where(m, scale[zp, pl.ds(e, 1), :], 0.0), axis=1, keepdims=True
                )
            picked = picked.astype(BF16)
            if r < 3:
                stage[a, zp, r] = picked
                xcopy(a, zp, r).start()
            else:
                rows[a][zp * PLANE + q, :, mine] = picked
                tcopy(a, zp * PLANE + q).start()

    def forward(a, zp):
        for r in range(3):
            b = zp * PLANE + mates[r]
            remote(
                stage.at[a, zp, r], rows[a].at[b, :, mine], xsend.at[a, zp, r],
                xrecv.at[a, b], partner,
            ).wait_recv()
            tcopy(a, b).start()

    def got(fn, a, s):
        for way in (1, -1):
            @pl.when(arrives(s, way))
            def _():
                fn(a, z - way * (s + 1))

    def vcopy(b):
        return remote(val.at[b, :, other], partner_in.at[b], vsend.at[b], vrecv.at[b], partner)

    def lanes(zp):
        return pl.ds(pl.multiple_of(zp * span, span), span)

    def sigmoid(v):
        return 1.0 / (1.0 + jnp.exp(-v))

    nt = (((1,), (1,)), ((), ()))
    tn = (((0,), (0,)), ((), ()))
    tile = 512 if width % 512 == 0 else width

    def group(zp):
        for j in range(PLANE):
            tarrive(0, zp * PLANE + j)
        x = tok[pl.ds(zp * PLANE, PLANE)].reshape(span, width)
        g = lax.dot_general(wg[...], x, nt, preferred_element_type=F32)
        u = lax.dot_general(wu[...], x, nt, preferred_element_type=F32)
        gate_act[zp] = g
        up_act[zp] = u
        h = (g * sigmoid(g) * u).astype(BF16)
        hid[:, lanes(zp)] = h
        for n in range(width // tile):
            cols = pl.ds(n * tile, tile)
            v = lax.dot_general(h, wd[:, cols], tn, preferred_element_type=F32)
            val[pl.ds(zp * PLANE, PLANE), :, cols] = v.astype(BF16).reshape(PLANE, pad, tile)
        for j in range(PLANE):
            vcopy(zp * PLANE + j).start()

    def grad_group(zp):
        for j in range(PLANE):
            tarrive(1, zp * PLANE + j)
        x = cot[pl.ds(zp * PLANE, PLANE)].reshape(span, width)
        hg = lax.dot_general(wd[...], x, nt, preferred_element_type=F32)
        g = gate_act[zp]
        s = sigmoid(g)
        ggrad[:, lanes(zp)] = (hg * up_act[zp] * s * (1.0 + g * (1.0 - s))).astype(BF16)
        ugrad[:, lanes(zp)] = (hg * g * s).astype(BF16)

    grads = ((ggrad, tok, wg), (ugrad, tok, wu), (hid, cot, wd))
    strip = 256 if width % 256 == 0 else width
    strips = width // strip

    def grad_strip(n, carry):
        cols = pl.ds(pl.multiple_of(n * strip, strip), strip)
        for left, right, out in grads:
            r = right[:, :, cols].reshape(experts * pad, strip)
            out[:, cols] = jnp.dot(left[...], r, preferred_element_type=F32).astype(BF16)
        return carry

    def bcopy(zp, r):
        return remote(
            back.at[zp, r], plane_in.at[zp, q], bsend.at[zp, r], brecv.at[zp, q],
            (z * PLANE + mates[r], c),
        )

    def give(zp):
        for r in (2, 0, 1, 3):
            b = zp * PLANE + (mates[r] if r < 3 else q)
            vcopy(b).wait_recv()
            total = (val[b, :, mine].astype(F32) + partner_in[b].astype(F32)).astype(BF16)
            if r < 3:
                back[zp, r] = total
                bcopy(zp, r).start()
            else:
                plane_in[zp, q] = total

    def combine(zp):
        for r in range(3):
            remote(
                back.at[zp, r], plane_in.at[zp, mates[r]], bsend.at[zp, r],
                brecv.at[zp, mates[r]], partner,
            ).wait_recv()
        total = jnp.zeros((sel_rows, half), F32)
        for j in range(PLANE):
            e = z * PLANE + j
            w = jnp.where(
                slot_id == side_ref[zp, pl.ds(e, 1), :],
                side_ref[zp, pl.ds(experts + e, 1), :],
                0.0,
            )
            high = w.astype(BF16)
            low = (w - high.astype(F32)).astype(BF16)
            both = jnp.concatenate([high, low], axis=0)
            values = plane_in[zp, j]
            total = total + lax.dot_general(
                both, jnp.concatenate([values, values], axis=0), tn, preferred_element_type=F32
            )
        acc[zp] = total

    def ucopy(w, s):
        to = d + (2 * w - 1) * PLANE
        return remote(
            out_stage.at[w, s], line_in.at[w, s], usend.at[w, s], urecv.at[w, s], (to, c)
        )

    def height(w):
        return z if w == 1 else line - 1 - z

    def lifts(w, s):
        return (height(w) <= s) & (height(w) < line - 1)

    def lands(w, s):
        return (height(w) > 0) & (height(w) - 1 <= s)

    zstart(0, 0)
    process(0, z)
    reward_copy.wait()
    scale[z] = sigmoid(part[0:1, :] + part_in[0:1, :]) * side_ref[z, experts : 2 * experts, :]
    last = line - 2
    for a in (0, 1):
        for s in range(line - 1):
            zwait(a, s)
            if a == 0 and s < last:
                zstart(a, s + 1)
            elif a == 0:
                loads[1].wait()
                lstart()
            got(process, a, s)
            if s == 0:
                forward(a, z)
            else:
                got(forward, a, s - 1)
            if a == 1:
                if s == last:
                    for i in range(line - 1):
                        give(order(i))
                    group(order(line - 1))
                else:
                    group(order(s + 1))
        if a == 0:
            process(1, z)
        got(forward, a, last)
        if a == 0:
            for cp in loads[2:5]:
                cp.wait()
            group(order(0))
    give(z)

    for i in range(line):
        grad_group(order(line - 1 - i))
    done = 0
    for s in range(line - 1):
        combine(order(s))
        if s > 0:
            for w in (1, 0):
                @pl.when(lands(w, s - 1))
                def _():
                    ucopy(w, s - 1).wait_recv()
        for w in (1, 0):
            blk = z + (2 * w - 1) * (line - 1 - s)

            @pl.when(lifts(w, s) & (height(w) > 0))
            def _():
                if s > 0:
                    out_stage[w, s] = (acc[blk] + line_in[w, s - 1].astype(F32)).astype(BF16)
                    ucopy(w, s).start()

            @pl.when(lifts(w, s) & (height(w) == 0))
            def _():
                out_stage[w, s] = acc[blk].astype(BF16)
                ucopy(w, s).start()
        upto = strips * (s + 1) // line
        lax.fori_loop(done, upto, grad_strip, 0)
        done = upto
    combine(z)
    lax.fori_loop(done, strips, grad_strip, 0)
    for w in (1, 0):
        @pl.when(lands(w, last))
        def _():
            ucopy(w, last).wait_recv()
            acc[z] = acc[z] + line_in[w, last].astype(F32)
    mixed_ref[...] = acc[z].astype(BF16)

    for b in range(experts):
        vcopy(b).wait_send()
        for a in (0, 1):
            tcopy(a, b).wait_send()
    for zp in range(line):
        for r in range(3):
            bcopy(zp, r).wait_send()
            for a in (0, 1):
                xcopy(a, zp, r).wait_send()
    for s in range(line - 1):
        for w in (1, 0):
            @pl.when(lifts(w, s))
            def _():
                ucopy(w, s).wait_send()

        for way in (1, -1):
            @pl.when(sends(0, s, way))
            def _():
                for cp in zcopies(0, s, way):
                    cp.wait_send()

            @pl.when(reaches(s + 1, way))
            def _():
                for cp in lcopy(s + 1, way):
                    cp.wait_send()


def vmem(count):
    return [pl.BlockSpec(memory_space=pltpu.VMEM)] * count


def hbm(count):
    return [pl.BlockSpec(memory_space=pl.ANY)] * count


DMA = pltpu.SemaphoreType.DMA


def planar(pool, select, reward_w, routes, gates, target, w_gate, w_up, w_down):
    dp = lax.axis_size("dp")
    line = dp // PLANE
    experts = dp * w_gate.shape[0]
    sel_rows, top = routes.shape
    capacity = 5 * sel_rows * top // (4 * experts)
    pad = -(-capacity // 16) * 16
    half = target.shape[1]
    units, width = w_gate.shape[1:]
    span = PLANE * pad
    grad_shape = pltpu.VMEM(w_gate.shape, BF16)
    rw = jnp.broadcast_to(reward_w[None, :], (16, half))
    slots = pltpu.VMEM((experts, pad, width), BF16)
    act = pltpu.VMEM((line, units, span), F32)
    flat = pltpu.VMEM((units, experts * pad), BF16)
    return pl.pallas_call(
        functools.partial(layer_kernel, line, pad),
        name="layer",
        out_shape=(pltpu.VMEM((sel_rows, half), BF16), grad_shape, grad_shape, grad_shape),
        in_specs=hbm(1) + vmem(2) + hbm(6),
        out_specs=tuple(vmem(4)),
        scratch_shapes=[
            pltpu.VMEM(pool.shape, BF16), pltpu.VMEM((top, sel_rows), jnp.int32),
            pltpu.VMEM((top, sel_rows), F32), slots, slots, act, act, flat, flat, flat, slots,
            pltpu.VMEM((2, line, sel_rows, half), BF16),
            pltpu.VMEM((line, 2 * experts, sel_rows), F32),
            pltpu.VMEM((line, experts, sel_rows), F32),
            pltpu.VMEM((16, sel_rows), F32),
            pltpu.VMEM((16, sel_rows), F32),
            pltpu.VMEM((2, line, 3, pad, half), BF16),
            pltpu.VMEM((experts, pad, half), BF16),
            pltpu.VMEM((line, 3, pad, half), BF16),
            pltpu.VMEM((line, PLANE, pad, half), BF16),
            pltpu.VMEM((line, sel_rows, half), F32),
            pltpu.VMEM((2, line - 1, sel_rows, half), BF16),
            pltpu.VMEM((2, line - 1, sel_rows, half), BF16),
            DMA((7,)),
            DMA((2, 2, line)), DMA((2, line)), DMA((2, line)), DMA((line,)),
            DMA((2, line)), DMA((line,)), DMA((2, line, 3)), DMA((2, experts)),
            DMA((2, experts)), DMA((2, experts)), DMA, DMA,
            DMA((experts,)), DMA((experts,)), DMA((line, 3)), DMA((line, PLANE)),
            DMA((2, line)), DMA((2, line)),
        ],
        compiler_params=pltpu.CompilerParams(
            collective_id=0, has_side_effects=True, vmem_limit_bytes=57 * 10**6
        ),
    )(pool, select.reshape(1, sel_rows), rw, routes.T, gates.T, target,
      w_gate, w_up, w_down)


def solution(mesh):
    in_specs = (
        P("dp", "tensor"), P("dp"), P("tensor"), P("dp", None), P("dp", None), P("dp", "tensor"),
        P("dp", "tensor", None), P("dp", "tensor", None), P("dp", "tensor", None),
    )
    out_specs = (
        P("dp", "tensor"), P("dp", "tensor", None), P("dp", "tensor", None),
        P("dp", "tensor", None),
    )
    dp, tensor = mesh.shape["dp"], mesh.shape["tensor"]
    fits = tensor == 2 and dp % (2 * PLANE) == 0
    local = planar if fits else generic
    return jax.shard_map(local, mesh=mesh, in_specs=in_specs, out_specs=out_specs, check_vma=False)
```

```python
import functools
import jax
import jax.numpy as jnp
from jax import lax
from jax.experimental import pallas as pl
from jax.experimental.pallas import tpu as pltpu
from jax.sharding import PartitionSpec as P

MESH = pl.DeviceIdType.MESH
PLANE = 4
F32 = jnp.float32
BF16 = jnp.bfloat16


def slot_factor(route_hit, weights):
    return jnp.sum(jnp.where(route_hit, weights.reshape(-1)[:, None], 0.0), axis=0)


def generic(pool, select, reward_w, routes, gates, target, w_gate, w_up, w_down):
    pool_rows = pool.shape[0]
    local_rows = select - lax.axis_index("dp") * pool_rows
    chosen = jnp.take(pool, local_rows, axis=0)
    sel_rows, top_count = routes.shape
    owners = lax.axis_size("dp")
    exp_dev = w_gate.shape[0]
    experts = owners * exp_dev
    capacity = 5 * sel_rows * top_count // (4 * experts)
    slot_count = experts * capacity
    flat_routes = routes.reshape(-1)
    onehot = (flat_routes[:, None] == jnp.arange(experts, dtype=jnp.int32)[None, :]).astype(
        jnp.int32
    )
    before = jnp.cumsum(onehot, axis=0) - onehot
    slot_rank = jnp.sum(before * onehot, axis=1)
    slot_place = flat_routes * capacity + slot_rank
    route_hit = slot_place[:, None] == jnp.arange(slot_count, dtype=jnp.int32)[None, :]
    route_pick = route_hit.astype(jnp.bfloat16).reshape(sel_rows, top_count, slot_count)
    token_pick = jnp.sum(route_pick, axis=1)
    reward = lax.psum(jnp.dot(chosen, reward_w, preferred_element_type=jnp.float32), "tensor")
    keep_scale = jax.nn.sigmoid(reward)
    slot_scale = slot_factor(route_hit, keep_scale[:, None] * gates)
    token_send = jnp.einsum(
        "sp,sd->pd", token_pick, chosen, preferred_element_type=jnp.float32
    ).astype(jnp.bfloat16)
    picked_target = jnp.einsum("sp,sd->pd", token_pick, target, preferred_element_type=jnp.float32)
    cot_send = (picked_target * slot_scale[:, None]).astype(jnp.bfloat16)
    token_part, cot_part = (
        lax.all_to_all(token_send, "dp", split_axis=0, concat_axis=0, tiled=True),
        lax.all_to_all(cot_send, "dp", split_axis=0, concat_axis=0, tiled=True),
    )
    received_tokens, received_cots = (
        lax.all_gather(token_part, "tensor", axis=1, tiled=True),
        lax.all_gather(cot_part, "tensor", axis=1, tiled=True),
    )
    width = received_tokens.shape[1]
    token_rows = received_tokens.reshape(owners, exp_dev, capacity, width)
    cot_rows = received_cots.reshape(owners, exp_dev, capacity, width)
    gate_act = jnp.einsum("secd,efd->secf", token_rows, w_gate, preferred_element_type=jnp.float32)
    up_act = jnp.einsum("secd,efd->secf", token_rows, w_up, preferred_element_type=jnp.float32)
    sigmoid_gate = jax.nn.sigmoid(gate_act)
    hidden = (gate_act * sigmoid_gate * up_act).astype(jnp.bfloat16)
    partial_value = jnp.einsum("secf,efd->secd", hidden, w_down, preferred_element_type=jnp.float32)
    summed = lax.psum_scatter(
        partial_value.astype(jnp.bfloat16), "tensor", scatter_dimension=3, tiled=True
    )
    returned = lax.all_to_all(summed, "dp", split_axis=0, concat_axis=0, tiled=True).reshape(
        slot_count, -1
    )
    route_rows = jnp.einsum("skp,pd->skd", route_pick, returned, preferred_element_type=jnp.float32)
    mixed = jnp.sum(route_rows * gates[:, :, None], axis=1).astype(jnp.bfloat16)
    hidden_grad = jnp.einsum("secd,efd->secf", cot_rows, w_down, preferred_element_type=jnp.float32)
    gate_grad = (
        hidden_grad * up_act * sigmoid_gate * (1.0 + gate_act * (1.0 - sigmoid_gate))
    ).astype(jnp.bfloat16)
    up_grad = (hidden_grad * gate_act * sigmoid_gate).astype(jnp.bfloat16)
    grad_down = jnp.einsum(
        "secf,secd->efd", hidden, cot_rows, preferred_element_type=jnp.float32
    ).astype(jnp.bfloat16)
    grad_gate = jnp.einsum(
        "secf,secd->efd", gate_grad, token_rows, preferred_element_type=jnp.float32
    ).astype(jnp.bfloat16)
    grad_up = jnp.einsum(
        "secf,secd->efd", up_grad, token_rows, preferred_element_type=jnp.float32
    ).astype(jnp.bfloat16)
    return (mixed, grad_gate, grad_up, grad_down)


def place(line):
    d = lax.axis_index("dp")
    c = lax.axis_index("tensor")
    z, q = d // PLANE, d % PLANE
    y, x = q // 2, q % 2
    mates = [((y + ry) % 2) * 2 + (x + rx) % 2 for ry, rx in ((0, 1), (1, 0), (1, 1))]
    return d, c, z, q, mates


def greet(d, c, z, q, mates, line):
    barrier = pltpu.get_barrier_semaphore()
    for m in mates:
        pl.semaphore_signal(barrier, inc=1, device_id=(z * PLANE + m, c), device_id_type=MESH)
    pl.semaphore_signal(barrier, inc=1, device_id=(d, 1 - c), device_id_type=MESH)

    @pl.when(z > 0)
    def _():
        pl.semaphore_signal(barrier, inc=1, device_id=(d - PLANE, c), device_id_type=MESH)

    @pl.when(z < line - 1)
    def _():
        pl.semaphore_signal(barrier, inc=1, device_id=(d + PLANE, c), device_id_type=MESH)


def greeted(z, line):
    below, above = (z + line - 1) // line, (2 * line - 2 - z) // line
    pl.semaphore_wait(pltpu.get_barrier_semaphore(), 4 + below + above)


def remote(src, dst, send, recv, dev):
    return pltpu.make_async_remote_copy(
        src_ref=src, dst_ref=dst, send_sem=send, recv_sem=recv, device_id=dev, device_id_type=MESH
    )


def layer_kernel(
    line, pad, pool_hbm, sel_ref, rw_ref, rt_ref, gt_ref, target_hbm, wg_hbm, wu_hbm, wd_hbm,
    mixed_ref, gg_ref, gu_ref, gd_ref,
    pool_ref, rt_vmem, gt_vmem, tok, cot, gate_act, up_act, hid, ggrad, ugrad, val,
    data, side_ref, scale, part, part_in, stage,
    partner_in, back, plane_in, acc, out_stage, line_in,
    lsem, zsend, zrecv, ssend, srecv, csend, crecv, xsend, xrecv, tsend, trecv, psend, precv,
    vsend, vrecv, bsend, brecv, usend, urecv,
):
    d, c, z, q, mates = place(line)
    experts = line * PLANE
    sel_rows, half = mixed_ref.shape
    top = gt_ref.shape[0]
    wg, wu, wd = gg_ref.at[0], gu_ref.at[0], gd_ref.at[0]
    units, width = wg.shape
    span = PLANE * pad
    rows = (tok, cot)
    mine = pl.ds(pl.multiple_of(c * half, half), half)
    other = pl.ds(pl.multiple_of((1 - c) * half, half), half)
    partner = (d, 1 - c)
    turn = 2 * (z // (line // 2)) - 1

    def order(i):
        return (z + turn * (1 + i) + 2 * line) % line

    greet(d, c, z, q, mates, line)
    loads = [
        pltpu.make_async_copy(src, dst, lsem.at[i])
        for i, (src, dst) in enumerate((
            (pool_hbm, pool_ref), (target_hbm, data.at[1, z]), (wg_hbm.at[0], wg),
            (wu_hbm.at[0], wu), (wd_hbm.at[0], wd), (rt_ref, rt_vmem), (gt_ref, gt_vmem),
        ))
    ]
    for i in (5, 6, 0, 1, 2, 3, 4):
        loads[i].start()

    loads[5].wait()
    loads[6].wait()
    expert_id = lax.broadcasted_iota(jnp.int32, (experts, sel_rows), 0)
    member = jnp.zeros((experts, sel_rows), F32)
    gate = jnp.zeros((experts, sel_rows), F32)
    for k in range(top):
        eq = rt_vmem[k : k + 1, :] == expert_id
        member = member + jnp.where(eq, 1.0, 0.0)
        gate = gate + jnp.where(eq, gt_vmem[k : k + 1, :], 0.0)
    tri = jnp.where(
        lax.broadcasted_iota(jnp.int32, (sel_rows, sel_rows), 0)
        < lax.broadcasted_iota(jnp.int32, (sel_rows, sel_rows), 1),
        1.0,
        0.0,
    ).astype(BF16)
    before = jnp.dot(member.astype(BF16), tri, preferred_element_type=F32)
    side_ref[z, 0:experts, :] = jnp.where(member > 0.5, before, -1.0)
    side_ref[z, experts : 2 * experts, :] = gate

    pool_rows = pool_ref.shape[0]
    hit = (
        lax.broadcasted_iota(jnp.int32, (pool_rows, sel_rows), 0) == sel_ref[...] - d * pool_rows
    ).astype(F32).astype(BF16)
    loads[0].wait()
    chosen = lax.dot_general(
        hit, pool_ref[...], (((0,), (0,)), ((), ())), preferred_element_type=F32
    ).astype(BF16)
    data[0, z] = chosen
    part[...] = lax.dot_general(
        rw_ref[...], chosen,
        (((1,), (1,)), ((), ())), preferred_element_type=F32,
    )

    greeted(z, line)
    reward_copy = remote(part, part_in, psend, precv, partner)
    reward_copy.start()

    def zcopies(a, s, way):
        blk = z - way * s
        dev = (d + way * PLANE, c)
        w = (way + 1) // 2
        main = remote(data.at[a, blk], data.at[a, blk], zsend.at[a, w, s], zrecv.at[a, blk], dev)
        if a == 0:
            extra = remote(
                side_ref.at[blk], side_ref.at[blk], ssend.at[w, s], srecv.at[blk], dev
            )
        else:
            extra = remote(scale.at[blk], scale.at[blk], csend.at[w, s], crecv.at[blk], dev)
        return extra, main

    def sends(a, s, way):
        blk, to = z - way * s, z + way
        return (blk >= 0) & (blk < line) & (to >= 0) & (to < line)

    def zstart(a, s):
        for way in (1, -1):
            @pl.when(sends(a, s, way))
            def _():
                for cp in zcopies(a, s, way):
                    cp.start()

    def arrives(s, way):
        blk = z - way * (s + 1)
        return (blk >= 0) & (blk < line)

    def zwait(a, s):
        for way in (1, -1):
            @pl.when(arrives(s, way))
            def _():
                blk = z - way * (s + 1)
                remote(
                    data.at[a, blk], data.at[a, blk], zsend.at[a, 0, 0], zrecv.at[a, blk], partner
                ).wait_recv()
                if a == 0:
                    remote(
                        side_ref.at[blk], side_ref.at[blk], ssend.at[0, 0], srecv.at[blk], partner
                    ).wait_recv()
                else:
                    remote(
                        scale.at[blk], scale.at[blk], csend.at[0, 0], crecv.at[blk], partner
                    ).wait_recv()

    def tcopy(a, b):
        spot = rows[a].at[b, :, mine]
        return remote(spot, spot, tsend.at[a, b], trecv.at[a, b], partner)

    def tarrive(a, b):
        spot = rows[a].at[b, :, other]
        remote(spot, spot, tsend.at[a, b], trecv.at[a, b], partner).wait_recv()

    def xcopy(a, zp, r):
        return remote(
            stage.at[a, zp, r],
            rows[a].at[zp * PLANE + q, :, mine],
            xsend.at[a, zp, r],
            xrecv.at[a, zp * PLANE + q],
            (z * PLANE + mates[r], c),
        )

    slot_id = lax.broadcasted_iota(jnp.int32, (pad, sel_rows), 0).astype(F32)

    def process(a, zp):
        block = data[a, zp]
        for r in (2, 0, 1, 3):
            e = z * PLANE + (mates[r] if r < 3 else q)
            m = slot_id == side_ref[zp, pl.ds(e, 1), :]
            picked = jnp.dot(
                jnp.where(m, 1.0, 0.0).astype(BF16), block, preferred_element_type=F32
            )
            if a == 1:
                picked = picked * jnp.sum(
                    jnp.where(m, scale[zp, pl.ds(e, 1), :], 0.0), axis=1, keepdims=True
                )
            picked = picked.astype(BF16)
            if r < 3:
                stage[a, zp, r] = picked
                xcopy(a, zp, r).start()
            else:
                rows[a][zp * PLANE + q, :, mine] = picked
                tcopy(a, zp * PLANE + q).start()

    def forward(a, zp):
        for r in range(3):
            b = zp * PLANE + mates[r]
            remote(
                stage.at[a, zp, r], rows[a].at[b, :, mine], xsend.at[a, zp, r],
                xrecv.at[a, b], partner,
            ).wait_recv()
            tcopy(a, b).start()

    def got(fn, a, s):
        for way in (1, -1):
            @pl.when(arrives(s, way))
            def _():
                fn(a, z - way * (s + 1))

    def vcopy(b):
        return remote(val.at[b, :, other], partner_in.at[b], vsend.at[b], vrecv.at[b], partner)

    def lanes(zp):
        return pl.ds(pl.multiple_of(zp * span, span), span)

    def sigmoid(v):
        return 1.0 / (1.0 + jnp.exp(-v))

    nt = (((1,), (1,)), ((), ()))
    tn = (((0,), (0,)), ((), ()))
    tile = 512 if width % 512 == 0 else width

    def group(zp):
        for j in range(PLANE):
            tarrive(0, zp * PLANE + j)
        x = tok[pl.ds(zp * PLANE, PLANE)].reshape(span, width)
        g = lax.dot_general(wg[...], x, nt, preferred_element_type=F32)
        u = lax.dot_general(wu[...], x, nt, preferred_element_type=F32)
        gate_act[zp] = g
        up_act[zp] = u
        h = (g * sigmoid(g) * u).astype(BF16)
        hid[:, lanes(zp)] = h
        for n in range(width // tile):
            cols = pl.ds(n * tile, tile)
            v = lax.dot_general(h, wd[:, cols], tn, preferred_element_type=F32)
            val[pl.ds(zp * PLANE, PLANE), :, cols] = v.astype(BF16).reshape(PLANE, pad, tile)
        for j in range(PLANE):
            vcopy(zp * PLANE + j).start()

    def grad_group(zp):
        for j in range(PLANE):
            tarrive(1, zp * PLANE + j)
        x = cot[pl.ds(zp * PLANE, PLANE)].reshape(span, width)
        hg = lax.dot_general(wd[...], x, nt, preferred_element_type=F32)
        g = gate_act[zp]
        s = sigmoid(g)
        ggrad[:, lanes(zp)] = (hg * up_act[zp] * s * (1.0 + g * (1.0 - s))).astype(BF16)
        ugrad[:, lanes(zp)] = (hg * g * s).astype(BF16)

    grads = ((ggrad, tok, wg), (ugrad, tok, wu), (hid, cot, wd))
    strip = 256 if width % 256 == 0 else width
    strips = width // strip

    def grad_strip(n, carry):
        cols = pl.ds(pl.multiple_of(n * strip, strip), strip)
        for left, right, out in grads:
            r = right[:, :, cols].reshape(experts * pad, strip)
            out[:, cols] = jnp.dot(left[...], r, preferred_element_type=F32).astype(BF16)
        return carry

    def bcopy(zp, r):
        return remote(
            back.at[zp, r], plane_in.at[zp, q], bsend.at[zp, r], brecv.at[zp, q],
            (z * PLANE + mates[r], c),
        )

    def give(zp):
        for r in (2, 0, 1, 3):
            b = zp * PLANE + (mates[r] if r < 3 else q)
            vcopy(b).wait_recv()
            total = (val[b, :, mine].astype(F32) + partner_in[b].astype(F32)).astype(BF16)
            if r < 3:
                back[zp, r] = total
                bcopy(zp, r).start()
            else:
                plane_in[zp, q] = total

    def combine(zp):
        for r in range(3):
            remote(
                back.at[zp, r], plane_in.at[zp, mates[r]], bsend.at[zp, r],
                brecv.at[zp, mates[r]], partner,
            ).wait_recv()
        total = jnp.zeros((sel_rows, half), F32)
        for j in range(PLANE):
            e = z * PLANE + j
            w = jnp.where(
                slot_id == side_ref[zp, pl.ds(e, 1), :],
                side_ref[zp, pl.ds(experts + e, 1), :],
                0.0,
            )
            high = w.astype(BF16)
            low = (w - high.astype(F32)).astype(BF16)
            both = jnp.concatenate([high, low], axis=0)
            values = plane_in[zp, j]
            total = total + lax.dot_general(
                both, jnp.concatenate([values, values], axis=0), tn, preferred_element_type=F32
            )
        acc[zp] = total

    def ucopy(w, s):
        to = d + (2 * w - 1) * PLANE
        return remote(
            out_stage.at[w, s], line_in.at[w, s], usend.at[w, s], urecv.at[w, s], (to, c)
        )

    def height(w):
        return z if w == 1 else line - 1 - z

    def lifts(w, s):
        return (height(w) <= s) & (height(w) < line - 1)

    def lands(w, s):
        return (height(w) > 0) & (height(w) - 1 <= s)

    zstart(0, 0)
    process(0, z)
    reward_copy.wait()
    scale[z] = sigmoid(part[0:1, :] + part_in[0:1, :]) * side_ref[z, experts : 2 * experts, :]
    last = line - 2
    for a in (0, 1):
        for s in range(line - 1):
            zwait(a, s)
            if s < last:
                zstart(a, s + 1)
            elif a == 0:
                loads[1].wait()
                zstart(1, 0)
            got(process, a, s)
            if s == 0:
                forward(a, z)
            else:
                got(forward, a, s - 1)
            if a == 1:
                if s == last:
                    for i in range(line - 1):
                        give(order(i))
                    group(order(line - 1))
                else:
                    group(order(s + 1))
        if a == 0:
            process(1, z)
        got(forward, a, last)
        if a == 0:
            for cp in loads[2:5]:
                cp.wait()
            group(order(0))
    give(z)

    for i in range(line):
        grad_group(order(line - 1 - i))
    done = 0
    for s in range(line - 1):
        combine(order(s))
        if s > 0:
            for w in (1, 0):
                @pl.when(lands(w, s - 1))
                def _():
                    ucopy(w, s - 1).wait_recv()
        for w in (1, 0):
            blk = z + (2 * w - 1) * (line - 1 - s)

            @pl.when(lifts(w, s) & (height(w) > 0))
            def _():
                if s > 0:
                    out_stage[w, s] = (acc[blk] + line_in[w, s - 1].astype(F32)).astype(BF16)
                    ucopy(w, s).start()

            @pl.when(lifts(w, s) & (height(w) == 0))
            def _():
                out_stage[w, s] = acc[blk].astype(BF16)
                ucopy(w, s).start()
        upto = strips * (s + 1) // line
        lax.fori_loop(done, upto, grad_strip, 0)
        done = upto
    combine(z)
    lax.fori_loop(done, strips, grad_strip, 0)
    for w in (1, 0):
        @pl.when(lands(w, last))
        def _():
            ucopy(w, last).wait_recv()
            acc[z] = acc[z] + line_in[w, last].astype(F32)
    mixed_ref[...] = acc[z].astype(BF16)

    for b in range(experts):
        vcopy(b).wait_send()
        for a in (0, 1):
            tcopy(a, b).wait_send()
    for zp in range(line):
        for r in range(3):
            bcopy(zp, r).wait_send()
            for a in (0, 1):
                xcopy(a, zp, r).wait_send()
    for s in range(line - 1):
        for w in (1, 0):
            @pl.when(lifts(w, s))
            def _():
                ucopy(w, s).wait_send()

        for a in (0, 1):
            for way in (1, -1):
                @pl.when(sends(a, s, way))
                def _():
                    for cp in zcopies(a, s, way):
                        cp.wait_send()


def vmem(count):
    return [pl.BlockSpec(memory_space=pltpu.VMEM)] * count


def hbm(count):
    return [pl.BlockSpec(memory_space=pl.ANY)] * count


DMA = pltpu.SemaphoreType.DMA


def planar(pool, select, reward_w, routes, gates, target, w_gate, w_up, w_down):
    dp = lax.axis_size("dp")
    line = dp // PLANE
    experts = dp * w_gate.shape[0]
    sel_rows, top = routes.shape
    capacity = 5 * sel_rows * top // (4 * experts)
    pad = -(-capacity // 16) * 16
    half = target.shape[1]
    units, width = w_gate.shape[1:]
    span = PLANE * pad
    grad_shape = pltpu.VMEM(w_gate.shape, BF16)
    rw = jnp.broadcast_to(reward_w[None, :], (16, half))
    slots = pltpu.VMEM((experts, pad, width), BF16)
    act = pltpu.VMEM((line, units, span), F32)
    flat = pltpu.VMEM((units, experts * pad), BF16)
    return pl.pallas_call(
        functools.partial(layer_kernel, line, pad),
        name="layer",
        out_shape=(pltpu.VMEM((sel_rows, half), BF16), grad_shape, grad_shape, grad_shape),
        in_specs=hbm(1) + vmem(2) + hbm(6),
        out_specs=tuple(vmem(4)),
        scratch_shapes=[
            pltpu.VMEM(pool.shape, BF16), pltpu.VMEM((top, sel_rows), jnp.int32),
            pltpu.VMEM((top, sel_rows), F32), slots, slots, act, act, flat, flat, flat, slots,
            pltpu.VMEM((2, line, sel_rows, half), BF16),
            pltpu.VMEM((line, 2 * experts, sel_rows), F32),
            pltpu.VMEM((line, experts, sel_rows), F32),
            pltpu.VMEM((16, sel_rows), F32),
            pltpu.VMEM((16, sel_rows), F32),
            pltpu.VMEM((2, line, 3, pad, half), BF16),
            pltpu.VMEM((experts, pad, half), BF16),
            pltpu.VMEM((line, 3, pad, half), BF16),
            pltpu.VMEM((line, PLANE, pad, half), BF16),
            pltpu.VMEM((line, sel_rows, half), F32),
            pltpu.VMEM((2, line - 1, sel_rows, half), BF16),
            pltpu.VMEM((2, line - 1, sel_rows, half), BF16),
            DMA((7,)),
            DMA((2, 2, line)), DMA((2, line)), DMA((2, line)), DMA((line,)),
            DMA((2, line)), DMA((line,)), DMA((2, line, 3)), DMA((2, experts)),
            DMA((2, experts)), DMA((2, experts)), DMA, DMA,
            DMA((experts,)), DMA((experts,)), DMA((line, 3)), DMA((line, PLANE)),
            DMA((2, line)), DMA((2, line)),
        ],
        compiler_params=pltpu.CompilerParams(
            collective_id=0, has_side_effects=True, vmem_limit_bytes=57 * 10**6
        ),
    )(pool, select.reshape(1, sel_rows), rw, routes.T, gates.T, target,
      w_gate, w_up, w_down)


def solution(mesh):
    in_specs = (
        P("dp", "tensor"), P("dp"), P("tensor"), P("dp", None), P("dp", None), P("dp", "tensor"),
        P("dp", "tensor", None), P("dp", "tensor", None), P("dp", "tensor", None),
    )
    out_specs = (
        P("dp", "tensor"), P("dp", "tensor", None), P("dp", "tensor", None),
        P("dp", "tensor", None),
    )
    dp, tensor = mesh.shape["dp"], mesh.shape["tensor"]
    fits = tensor == 2 and dp % (2 * PLANE) == 0
    local = planar if fits else generic
    return jax.shard_map(local, mesh=mesh, in_specs=in_specs, out_specs=out_specs, check_vma=False)
```
